32 devices in a mesh: groups: 2 (over x), blk: 8 (over z, y), head: 2 (over core).
Axes of the slice: x: 2, y: 2, z: 4, core: 2. Of those that a mesh axis runs over, the one named last changes fastest.
Arguments:
- queries: bfloat16 [2048, 40, 128], P(('groups', 'blk', 'head')), parts along dimension 0, may hold values from -25 to 25
- keys: bfloat16 [2048, 8, 128], P(('groups', 'blk', 'head')), parts along dimension 0, may hold values from -5 to 5
- values: bfloat16 [2048, 8, 128], P(('groups', 'blk', 'head')), parts along dimension 0, may hold values from -6 to 6
- out_grad: bfloat16 [2048, 40, 128], P(('groups', 'blk', 'head')), parts along dimension 0, may hold values from -6 to 6
- block_list: int32 [16, 4], P(('groups', 'blk')), parts along dimension 0, may hold values from -1 to 7, as said below
- positions: int32 [2048], P(('groups', 'blk', 'head')), parts along dimension 0, may hold values from 0 to 511, as said below
Outputs:
- attention_out: bfloat16 [2048, 40, 128], P(('groups', 'blk', 'head')), parts along dimension 0
- query_grad: bfloat16 [2048, 40, 128], P(('groups', 'blk', 'head')), parts along dimension 0
- key_grad: bfloat16 [2048, 8, 128], P(('groups', 'blk', 'head')), parts along dimension 0
- value_grad: bfloat16 [2048, 8, 128], P(('groups', 'blk', 'head')), parts along dimension 0
The draws below stay inside these ranges and needn't reach their ends.
There are 2 independent parts, one for each index of `groups`. The reference program is written for one: setup_inputs(seed, part) draws one part's arguments, and reference() takes and returns one part's arrays. A program takes and returns all parts, laid end to end along the dimension named above; each array names one. Nothing has to cross between parts.
Inputs may be any that keep to these rules, and one draw needn't show every extreme that they name: `block_list`: row b lists the mask blocks whose keys the queries of block b see: the ancestors of block b in the rollout tree and b itself, in order of depth from the root, then -1 entries. Every listed block is at most b, the list of b's parent is the start of b's list, and at least one row holds 4 blocks. `positions`: the position of token t is 128 times (the number of listed blocks in the row of its block, minus one) plus t mod 128.
All inputs are finite; a program needn't handle non-finite values.
Results may differ from the reference program's by a relative error of at most 0.02.
The reference program's roundings to bfloat16 on the way count: a program that leaves them out, or rounds other values in their place, can miss the bound.
Values may be sent and summed in bfloat16 or wider, within the bound.
A program may use at most 128 MiB of HBM per device.

```python
import math
import jax
import jax.numpy as jnp
from jax import lax

H = 40
KVH = 8
DH = 128
BLOCK = 128
RB = 1
NQB = 8
TOKENS = 1024
KB = 4
N_BLK = 8


def tree_tables(key):
    base = jax.random.fold_in(key, 7)
    picks = jax.random.randint(base, (NQB,), 0, 1 << 20)
    columns = jnp.arange(KB, dtype=jnp.int32)

    def grow(carry, block):
        lists, depths = carry
        spine = block < KB
        chosen = jnp.where(block > 0, picks[block] % jnp.maximum(block, 1), 0)
        chosen = jnp.where(spine, block - 1, chosen)
        safe_chosen = jnp.maximum(chosen, 0)
        chosen_depth = depths[safe_chosen]
        capped = chosen_depth >= KB - 1
        parent = jnp.where(capped, lists[safe_chosen, KB - 2], safe_chosen)
        parent_depth = jnp.where(capped, KB - 2, chosen_depth)
        own_depth = jnp.where(block == 0, 0, parent_depth + 1)
        parent_row = lists[jnp.maximum(parent, 0)]
        row = jnp.where(columns < own_depth, parent_row, -1)
        row = jnp.where(columns == own_depth, block, row)
        lists = lists.at[block].set(row)
        depths = depths.at[block].set(own_depth)
        return ((lists, depths), block)
    start = (jnp.full((NQB, KB), -1, jnp.int32), jnp.zeros((NQB,), jnp.int32))
    (lists, depths), visited = lax.scan(grow, start, jnp.arange(NQB, dtype=jnp.int32))
    return (lists, depths)


def draw_block_list(key, part):
    lists, depths = tree_tables(key)
    return lists


def draw_positions(key, part):
    lists, depths = tree_tables(key)
    token = jnp.arange(TOKENS, dtype=jnp.int32)
    return depths[token // BLOCK] * BLOCK + token % BLOCK


def key_field(key):
    base = jax.random.fold_in(key, 21)
    field = jnp.clip(1.5 * jax.random.normal(base, (TOKENS, KVH, DH), jnp.float32), -5.0, 5.0)
    return field


def draw_keys(key, part):
    return key_field(key).astype(jnp.bfloat16)


def draw_queries(key, part):
    base = jax.random.fold_in(key, 22)
    field = jnp.clip(1.5 * jax.random.normal(base, (TOKENS, H, DH), jnp.float32), -6.0, 6.0)
    return field.astype(jnp.bfloat16)


def shard_levels(own_key, shape, split, smallest, top_value):
    def one(position, parts):
        steps = jax.random.uniform(jax.random.fold_in(jax.random.fold_in(own_key, 6), position), (parts,), jnp.float32, smallest / len(split), top_value / len(split))
        return jnp.repeat(jnp.exp(steps), shape[position] // parts).reshape((-1,) + (1,) * (len(shape) - position - 1))

    gain = one(*split[0])
    for cut in split[1:]:
        gain = gain * one(*cut)
    return gain


def normal_values(own_key, extent, spread, limit, split=(), kind=jnp.bfloat16):
    values = jax.random.normal(own_key, extent, jnp.float32) * spread
    if len(split) > 0:
        values = shard_levels(own_key, extent, split, -0.22, 0.18) * values
    return jnp.clip(values, min=-limit, max=limit).astype(kind)


def setup_inputs(seed: int = 0, part: int = 0) -> dict:
    key_list = jax.random.split(jax.random.key(seed), 7)
    part_keys = jax.random.split(jax.random.fold_in(key_list[6], part), 7)
    return {
        "queries": draw_queries(jax.random.fold_in(jax.random.fold_in(key_list[6], part), 71), part),
        "keys": draw_keys(jax.random.fold_in(jax.random.fold_in(key_list[6], part), 71), part),
        "values": normal_values(part_keys[2], (TOKENS, KVH, DH), 1.0, 6.0, ((0, 16),)),
        "out_grad": normal_values(part_keys[3], (TOKENS, H, DH), 1.0, 6.0, ((0, 16),)),
        "block_list": draw_block_list(jax.random.fold_in(jax.random.fold_in(key_list[6], part), 71), part),
        "positions": draw_positions(jax.random.fold_in(jax.random.fold_in(key_list[6], part), 71), part),
    }


ROPE_BASE = 10000.0
NEG_FILL = -1e+30

def rotate(tensor, place, sign):
    half = tensor.shape[-1] // 2
    exponent = 2.0 * jnp.arange(half, dtype=jnp.float32) / tensor.shape[-1]
    frequency = ROPE_BASE ** (-exponent)
    angle = sign * place.astype(jnp.float32)[:, None] * frequency[None, :]
    cosine = jnp.cos(angle)[:, None, :]
    sine = jnp.sin(angle)[:, None, :]
    first = tensor[..., :half]
    second = tensor[..., half:]
    return jnp.concatenate([first * cosine - second * sine, second * cosine + first * sine], axis=-1)

def narrowed(tensor):
    return lax.optimization_barrier(tensor.astype(jnp.bfloat16)).astype(jnp.float32)

def reference(queries, keys, values, out_grad, block_list, positions):
    group = H // KVH
    scale = 1.0 / math.sqrt(DH)
    rows = RB * BLOCK
    rotated_query = rotate(queries.astype(jnp.float32), positions, 1.0).astype(jnp.bfloat16)
    rotated_key = rotate(keys.astype(jnp.float32), positions, 1.0).astype(jnp.bfloat16)
    key_full = rotated_key.astype(jnp.float32)
    value_full = values.astype(jnp.float32)
    token_index = jnp.arange(TOKENS, dtype=jnp.int32)
    key_block = token_index // BLOCK
    listed = jnp.any(block_list[:, :, None] == jnp.arange(NQB, dtype=jnp.int32)[None, None, :], axis=1)

    def per_rank(carry, rank):
        grad_keys, grad_values = carry
        start = (rank * rows).astype(jnp.int32)
        query_tiles = lax.dynamic_slice_in_dim(rotated_query, start, rows, 0).astype(jnp.float32).reshape(rows, KVH, group, DH)
        grad_tiles = lax.dynamic_slice_in_dim(out_grad, start, rows, 0).astype(jnp.float32).reshape(rows, KVH, group, DH)
        query_index = start + jnp.arange(rows, dtype=jnp.int32)
        query_block = query_index // BLOCK
        seen = listed[query_block][:, key_block]
        causal = (key_block[None, :] != query_block[:, None]) | (token_index[None, :] <= query_index[:, None])
        mask = (seen & causal)[:, None, None, :]
        score = jnp.einsum('tkgd,skd->tkgs', query_tiles, key_full) * scale
        score = jnp.where(mask, score, NEG_FILL)
        best = lax.optimization_barrier(jnp.max(score, axis=-1))
        unscaled = jnp.where(mask, jnp.exp(score - best[..., None]), 0.0)
        total = lax.optimization_barrier(jnp.sum(unscaled, axis=-1))
        log_total = best + jnp.log(total)
        attended = jnp.einsum('tkgs,skd->tkgd', narrowed(unscaled), value_full) / total[..., None]
        out_tiles = attended.astype(jnp.bfloat16)
        delta = lax.optimization_barrier(jnp.sum(grad_tiles * out_tiles.astype(jnp.float32), axis=-1))
        probability = jnp.where(mask, jnp.exp(score - log_total[..., None]), 0.0)
        value_term = jnp.einsum('tkgs,tkgd->skd', narrowed(probability), grad_tiles)
        prob_grad = jnp.einsum('tkgd,skd->tkgs', grad_tiles, value_full)
        score_grad = narrowed(probability * (prob_grad - delta[..., None]))
        grad_query = jnp.einsum('tkgs,skd->tkgd', score_grad, key_full) * scale
        key_term = jnp.einsum('tkgs,tkgd->skd', score_grad, query_tiles) * scale
        grad_keys = grad_keys + narrowed(key_term)
        grad_values = grad_values + narrowed(value_term)
        return ((grad_keys, grad_values), (out_tiles.reshape(rows, H, DH), grad_query.reshape(rows, H, DH)))
    empty = jnp.zeros((TOKENS, KVH, DH), jnp.float32)
    (grad_keys, grad_values), (out_rows, grad_rows) = lax.scan(per_rank, (empty, empty), jnp.arange(N_BLK, dtype=jnp.int32))
    attention_out = out_rows.reshape(TOKENS, H, DH)
    query_grad = rotate(grad_rows.reshape(TOKENS, H, DH), positions, -1.0).astype(jnp.bfloat16)
    key_grad = rotate(grad_keys, positions, -1.0).astype(jnp.bfloat16)
    value_grad = grad_values.astype(jnp.bfloat16)
    return (attention_out, query_grad, key_grad, value_grad)
```

```python
import functools
import math

import jax
import jax.numpy as jnp
import numpy as np
from jax import lax
from jax.experimental import pallas as pl
from jax.experimental.pallas import tpu as pltpu
from jax.sharding import PartitionSpec as P

BLOCK = 128
ROPE_BASE = 10000.0
NEG_FILL = -1e30
LAG = 4
SKEW = 4
EARLY = ()


def tables(place, width):
    half = width // 2
    exponent = 2.0 * jnp.arange(half, dtype=jnp.float32) / width
    frequency = ROPE_BASE ** (-exponent)
    angle = place.astype(jnp.float32)[:, None] * frequency[None, :]
    cosine, sine = jnp.cos(angle), jnp.sin(angle)
    return jnp.concatenate([cosine, cosine], -1), jnp.concatenate([-sine, sine], -1)


def flow_kernel(
    blocks, inner, width, group, scale,
    list_ref, q_raw, k_raw, v_raw, g_raw, cos_ref, sin_ref, out_raw, qg_raw, kg_raw, vg_raw, *scratch,
):
    tokens, heads, depth = q_raw.shape
    heads = heads // 2
    key_heads = k_raw.shape[1] // 2
    outer = blocks // inner
    rows = group * BLOCK
    f32, low = jnp.float32, jnp.bfloat16
    nt = (((1,), (1,)), ((), ()))
    kv = scratch[:key_heads]
    (q_in, g_in, kv_in, out_home, qg_home, kvg_home, q_full, g_full, out_full, qg_full, kvg, k_all, v_all, part, own, y_send, y_part, z_send, z_part, acc, total_kv,
     core_send, core_recv, gz_send, gz_recv, gy_send, gy_recv, ry_send, ry_recv, rz_send, rz_recv) = scratch[key_heads:]

    me = lax.axis_index("blk")
    core = lax.axis_index("head")
    other = 1 - core
    z, y = me // inner, me % inner
    up, down = {"blk": me + inner}, {"blk": me - inner}
    side = {"blk": z * inner + (inner - 1 - y)}
    twin = {"head": other}
    mesh_id = pl.DeviceIdType.MESH
    mine = pl.ds(pl.multiple_of(core * tokens, tokens), tokens)
    theirs = pl.ds(pl.multiple_of(other * tokens, tokens), tokens)

    def remote(source, target, send, recv, device):
        return pltpu.make_async_remote_copy(
            src_ref=source, dst_ref=target, send_sem=send, recv_sem=recv, device_id=device, device_id_type=mesh_id
        )

    def repeat(count, step):
        if count <= 4:
            for index in range(count):
                step(index)
        else:
            lax.fori_loop(0, count, lambda index, carry: (step(index), carry)[1], 0)

    barrier = pltpu.get_barrier_semaphore()
    pl.semaphore_signal(barrier, inc=1, device_id=twin, device_id_type=mesh_id)
    if inner > 1:
        pl.semaphore_signal(barrier, inc=1, device_id=side, device_id_type=mesh_id)

    @pl.when(z > 0)
    def _():
        pl.semaphore_signal(barrier, inc=1, device_id=down, device_id_type=mesh_id)

    @pl.when(z < outer - 1)
    def _():
        pl.semaphore_signal(barrier, inc=1, device_id=up, device_id_type=mesh_id)

    peers = (2 if inner > 1 else 1) + (z + outer - 1) // outer + (2 * outer - 2 - z) // outer
    pl.semaphore_wait(barrier, peers)

    half = depth // 2
    step_tokens = 16

    def turn(x, place, sign):
        cosine, sine = cos_ref[place, :], sin_ref[place, :]
        swapped = pltpu.roll(x, half, x.ndim - 1)
        return x * cosine[None] + swapped * (sign * sine)[None]

    def bring(raw, write, rotate):
        for start in range(0, tokens, step_tokens):
            x = jnp.transpose(raw[start : start + step_tokens].astype(f32), (1, 0, 2))
            if rotate:
                place = pl.ds(pl.multiple_of(core * tokens + start, step_tokens), step_tokens)
                x = turn(x, place, 1.0)
            write(slice(start, start + step_tokens), x.astype(low))

    def take(read, raw):
        for start in range(0, tokens, step_tokens):
            x = read(slice(start, start + step_tokens)).astype(f32)
            raw[start : start + step_tokens] = jnp.transpose(x, (1, 0, 2)).astype(low)

    def write_to(ref, lane=None):
        def write(place, x):
            if lane is None:
                ref[:, place, :] = x
            else:
                ref[:, lane, place, :] = x

        return write

    bring(k_raw, write_to(kv_in, 0), True)
    bring(v_raw, write_to(kv_in, 1), False)
    swaps = []
    for h in range(key_heads):
        swaps.append(
            remote(kv_in.at[other * key_heads + h], kv[h].at[me, :, mine, :], core_send.at[h], core_recv.at[h], twin)
        )
    k = key_heads
    swaps.append(
        remote(q_in.at[pl.ds(other * heads, heads)], q_full.at[:, mine, :], core_send.at[k], core_recv.at[k], twin)
    )
    swaps.append(
        remote(g_in.at[pl.ds(other * heads, heads)], g_full.at[:, mine, :], core_send.at[k + 1], core_recv.at[k + 1], twin)
    )
    for copy in swaps[:key_heads]:
        copy.start()
    for h in range(key_heads):
        kv[h][me, :, mine, :] = kv_in[core * key_heads + h]

    def bring_queries():
        bring(q_raw, write_to(q_in), True)
        swaps[key_heads].start()
        bring(g_raw, write_to(g_in), False)
        swaps[key_heads + 1].start()
        q_full[:, mine, :] = q_in[pl.ds(core * heads, heads)]
        g_full[:, mine, :] = g_in[pl.ds(core * heads, heads)]
        part[width] = jnp.zeros(part.shape[1:], part.dtype)

    def early(h):
        return inner > 1 and h in EARLY

    def lanes(h):
        return 2 if early(h) else 1

    def column(lane):
        return y if lane == 0 else inner - 1 - y

    def gather_z(s, h, lane):
        view = kv[h].at[(z - s) * inner + column(lane)]
        return remote(view, view, gz_send.at[s, h, lane], gz_recv.at[s, h, lane], up)

    def arrived_z(s, h, lane):
        view = kv[h].at[(z - s) * inner + column(lane)]
        return remote(view, view, gz_send.at[s - 1, h, lane], gz_recv.at[s - 1, h, lane], down)

    def gather_y(s, h):
        view = kv[h].at[(z - s) * inner + column(0)]
        return remote(view, view, gy_send.at[s, h], gy_recv.at[s, h], side)

    def arrived_y(s, h):
        view = kv[h].at[(z - s) * inner + column(1)]
        return remote(view, view, gy_send.at[s, h], gy_recv.at[s, h], side)

    def crosses(s, h):
        return inner > 1 and (s == 0 or not early(h))

    def sends_y(s, h):
        return (z >= s) & (y == 0) if s == 0 and not early(h) else z >= s

    def takes_y(s, h):
        return (z >= s) & (y == 1) if s == 0 and not early(h) else z >= s

    def forward(s, h):
        if s == 0:
            swaps[h].wait_recv()
            if early(h):
                gather_y(0, h).start()
        for lane in range(lanes(h)):
            if s > 0:

                @pl.when(z >= s)
                def _():
                    arrived_z(s, h, lane).wait_recv()

            elif lane == 1:
                arrived_y(0, h).wait_recv()

            @pl.when((z >= s) & (z < outer - 1))
            def _():
                gather_z(s, h, lane).start()

        if crosses(s, h) and not early(h):

            @pl.when(sends_y(s, h))
            def _():
                gather_y(s, h).start()

    def attend(h):
        if inner > 1 and not early(h):
            for s in range(outer):

                @pl.when(takes_y(s, h))
                def _():
                    arrived_y(s, h).wait_recv()

        if h == 0:
            swaps[key_heads].wait_recv()
            swaps[key_heads + 1].wait_recv()
        first = h * group
        for entry in range(width):
            block = jnp.maximum(list_ref[entry], 0)
            k_all[pl.ds(entry * BLOCK, BLOCK), :] = kv[h][block, 0]
            v_all[pl.ds(entry * BLOCK, BLOCK), :] = kv[h][block, 1]
        q = q_full[pl.ds(first, group)].reshape(rows, depth)
        g = g_full[pl.ds(first, group)].reshape(rows, depth)
        kk, vv = k_all[...], v_all[...]
        score = lax.dot_general(kk, q, nt, preferred_element_type=f32) * scale
        prob_grad = lax.dot_general(vv, g, nt, preferred_element_type=f32)
        key_row = lax.broadcasted_iota(jnp.int32, (BLOCK, rows), 0)
        query_row = lax.broadcasted_iota(jnp.int32, (BLOCK, rows), 1) % BLOCK
        causal = key_row <= query_row
        pieces = []
        for entry in range(width):
            block = list_ref[entry]
            allowed = jnp.logical_and(block >= 0, jnp.logical_or(block != me, causal))
            pieces.append(jnp.where(allowed, score[entry * BLOCK : (entry + 1) * BLOCK], NEG_FILL))
        score = jnp.concatenate(pieces, axis=0)
        best = jnp.max(score, axis=0, keepdims=True)
        weights = jnp.exp(score - best)
        inverse = 1.0 / jnp.sum(weights, axis=0, keepdims=True)
        out_t = jnp.dot(vv.T, weights.astype(low), preferred_element_type=f32) * inverse
        out_low = out_t.astype(low)
        out_full[pl.ds(first, group)] = out_t.T.astype(low).reshape(group, BLOCK, depth)
        delta = jnp.sum(g.astype(f32).T * out_low.astype(f32), axis=0, keepdims=True)
        prob = weights * inverse
        score_grad = (prob * (prob_grad - delta)).astype(low)
        value_part = jnp.dot(prob.astype(low), g, preferred_element_type=f32).astype(low)
        key_part = (jnp.dot(score_grad, q, preferred_element_type=f32) * scale).astype(low)
        for entry in range(width):
            part[entry, 0] = key_part[entry * BLOCK : (entry + 1) * BLOCK]
            part[entry, 1] = value_part[entry * BLOCK : (entry + 1) * BLOCK]

        def place(block):
            slot = jnp.int32(width)
            for entry in range(width):
                slot = jnp.where(list_ref[entry] == block, entry, slot)
            return slot

        def spread(zd):
            if inner > 1 and not early(h):

                @pl.when((zd < z) | ((zd == z) & (y == 1)))
                def _():
                    y_send[h, zd] = part[place(zd * inner + column(1))]
                    reduce_y(zd, h).start()

            for lane in range(lanes(h)):
                own[h, zd, lane] = part[place(zd * inner + column(lane))]

        repeat(outer, spread)
        qg = (jnp.dot(kk.T, score_grad, preferred_element_type=f32) * scale).T
        qg = qg.reshape(group, BLOCK, depth)
        half = depth // 2
        swapped = jnp.concatenate([qg[..., half:], qg[..., :half]], axis=-1)
        qg_full[pl.ds(first, group)] = (qg * cos_ref[...][None] - swapped * sin_ref[...][None]).astype(low)
        for copy in homeward(h):
            copy.start()
        out_home[pl.ds(core * heads + first, group)] = out_full[pl.ds(first, group), mine, :]
        qg_home[pl.ds(core * heads + first, group)] = qg_full[pl.ds(first, group), mine, :]

    def homeward(h):
        source, target = pl.ds(h * group, group), pl.ds(core * heads + h * group, group)
        a, b = key_heads + 2 + h, 2 * key_heads + 2 + h
        return (
            remote(out_full.at[source, theirs, :], out_home.at[target], core_send.at[a], core_recv.at[a], twin),
            remote(qg_full.at[source, theirs, :], qg_home.at[target], core_send.at[b], core_recv.at[b], twin),
        )

    def reduce_y(zd, h):
        return remote(y_send.at[h, zd], y_part.at[h, zd], ry_send.at[zd, h], ry_recv.at[zd, h], side)

    def reduce_z(zd, h, lane):
        return remote(
            z_send.at[h, zd, lane], z_part.at[h, zd, lane], rz_send.at[zd, h, lane], rz_recv.at[zd, h, lane], down
        )

    def reduce(h):
        def one(zd):
            for lane in reversed(range(lanes(h))):

                @pl.when(zd <= z)
                def _():
                    acc[...] = own[h, zd, lane].astype(f32)

                    if inner > 1 and not early(h):

                        @pl.when((zd < z) | (y == 0))
                        def _():
                            reduce_y(zd, h).wait_recv()
                            acc[...] += y_part[h, zd].astype(f32)

                    @pl.when(z < outer - 1)
                    def _():
                        reduce_z(zd, h, lane).wait_recv()
                        acc[...] += z_part[h, zd, lane].astype(f32)

                    @pl.when(zd < z)
                    def _():
                        z_send[h, zd, lane] = acc[...].astype(low)
                        reduce_z(zd, h, lane).start()

                    @pl.when(zd == z)
                    def _():
                        if lane == 1:
                            y_send[h, zd] = acc[...].astype(low)
                            reduce_y(zd, h).start()
                        else:
                            total_kv[h] = acc[...]

        repeat(outer, one)

    def settle(h):
        if early(h):
            reduce_y(z, h).wait_recv()
            total_kv[h] += y_part[h, z].astype(f32)

    moves = sorted((h + SKEW * s, s, h) for h in range(key_heads) for s in range(outer))
    ends = [moves.index((h + SKEW * (outer - 1), outer - 1, h)) for h in range(key_heads)]
    ready = [min(end + LAG, len(moves) - 1) for end in ends]
    for step, (_, s, h) in enumerate(moves):
        forward(s, h)
        if step == key_heads - 1:
            bring_queries()
        for done in range(key_heads):
            if ready[done] == step:
                attend(done)
                if done >= 1:
                    reduce(done - 1)
    for h in range(key_heads):
        for copy in homeward(h):
            copy.wait()
    take(lambda place: out_home[:, place, :], out_raw)
    take(lambda place: qg_home[:, place, :], qg_raw)
    reduce(key_heads - 1)
    for h in range(key_heads):
        settle(h)

    key_total = total_kv[:, 0]
    half = depth // 2
    swapped = jnp.concatenate([key_total[..., half:], key_total[..., :half]], axis=-1)
    kvg[:, 0] = (key_total * cos_ref[...][None] - swapped * sin_ref[...][None]).astype(low)
    kvg[:, 1] = total_kv[:, 1].astype(low)
    final = 3 * key_heads + 2
    target = pl.ds(core * key_heads, key_heads)
    closing = remote(kvg.at[:, :, theirs, :], kvg_home.at[target], core_send.at[final], core_recv.at[final], twin)
    closing.start()
    kvg_home[target] = kvg[:, :, mine, :]

    for copy in swaps:
        copy.wait_send()
    for h in range(key_heads):
        for s in range(outer):

            for lane in range(lanes(h)):

                @pl.when((z >= s) & (z < outer - 1))
                def _():
                    gather_z(s, h, lane).wait_send()

                @pl.when(s < z)
                def _():
                    reduce_z(s, h, lane).wait_send()

            if crosses(s, h):

                @pl.when(sends_y(s, h))
                def _():
                    gather_y(s, h).wait_send()

            if inner > 1 and not early(h):

                @pl.when((s < z) | ((s == z) & (y == 1)))
                def _():
                    reduce_y(s, h).wait_send()

        if early(h):
            reduce_y(z, h).wait_send()
    closing.wait()
    take(lambda place: kvg_home[:, 0, place, :], kg_raw)
    take(lambda place: kvg_home[:, 1, place, :], vg_raw)


def flow(blocks, list_row, q, k, v, g, cosine, sine):
    tokens, heads, depth = q.shape
    key_heads = k.shape[1] // 2
    group = heads // k.shape[1]
    width = list_row.shape[0]
    inner = 2 if blocks == 8 else 1
    outer = blocks // inner
    low, f32 = jnp.bfloat16, jnp.float32
    vmem, dma = pltpu.VMEM, pltpu.SemaphoreType.DMA
    whole = pl.BlockSpec(memory_space=pltpu.VMEM)
    half_heads = (heads // 2, BLOCK, depth)
    tile = (2, BLOCK, depth)
    sided = (key_heads, outer if inner > 1 else 1) + tile
    flags = (outer, key_heads)
    scratch = [vmem((blocks,) + tile, low)] * key_heads
    home = [vmem((heads, tokens, depth), low)] * 2 + [vmem((2 * key_heads, 2, tokens, depth), low)]
    scratch += home + home + [vmem(half_heads, low)] * 4
    scratch += [vmem((key_heads,) + tile, low)]
    scratch += [vmem((width * BLOCK, depth), low)] * 2
    scratch += [vmem((width + 1,) + tile, low)]
    scratch += [vmem((key_heads, outer, inner) + tile, low)]
    scratch += [vmem(sided, low)] * 2
    scratch += [vmem((key_heads, outer, inner) + tile, low)] * 2
    scratch += [vmem(tile, f32), vmem((key_heads,) + tile, f32)]
    scratch += [dma((3 * key_heads + 3,))] * 2
    scratch += [dma(flags + (inner,))] * 2 + [dma(flags)] * 4 + [dma(flags + (inner,))] * 2
    return pl.pallas_call(
        functools.partial(flow_kernel, blocks, inner, width, group, 1.0 / math.sqrt(depth)),
        in_specs=[pl.BlockSpec(memory_space=pltpu.SMEM)] + [whole] * 6,
        out_specs=[whole] * 4,
        out_shape=[jax.ShapeDtypeStruct(x.shape, low) for x in (q, q, k, k)],
        scratch_shapes=scratch,
        compiler_params=pltpu.CompilerParams(
            collective_id=0, has_side_effects=True, vmem_limit_bytes=60 << 20
        ),
        name="flow",
    )(list_row, q, k, v, g, cosine, sine)


def quad_kernel(
    outer, width, group, scale,
    list_ref, place_ref, k_raw, v_raw, token_ref, base_ref, q_far, g_far, out_raw, qg_raw, kg_raw, vg_raw, *scratch,
):
    tokens, key_heads, depth = k_raw.shape
    local = key_heads // 4
    heads = local * group
    rows = group * BLOCK
    f32, low = jnp.float32, jnp.bfloat16
    nt = (((1,), (1,)), ((), ()))
    kv = scratch[:local]
    (q_raw, g_raw, kv_in, q_in, g_in, q_full, g_full, out_full, qg_full, out_home, qg_home, kvg, kvg_home, k_all, v_all, part,
     own, z_send, z_part, acc, cos_ref, sin_ref, note,
     far_sem, note_send, note_recv, kv_send, kv_recv, q_send, q_recv, g_send, g_recv, out_send, out_recv, qg_send, qg_recv,
     home_send, home_recv, gz_send, gz_recv, rz_send, rz_recv) = scratch[local:]

    me = lax.axis_index("blk")
    core = lax.axis_index("head")
    z, y = me // 2, me % 2
    quarter = 2 * y + core
    mesh_id = pl.DeviceIdType.MESH
    mine = pl.ds(pl.multiple_of(core * tokens, tokens), tokens)
    theirs = pl.ds(pl.multiple_of((1 - core) * tokens, tokens), tokens)
    half = depth // 2
    step_tokens = 16

    def row_of(side):
        return y if side == 0 else 1 - y

    def core_of(cross):
        return core if cross == 0 else 1 - core

    def peer(side, cross):
        return {"blk": 2 * z + row_of(side), "head": core_of(cross)}

    def quarter_of(side, cross):
        return 2 * row_of(side) + core_of(cross)

    def level(other):
        return {"blk": 2 * other + y}

    def remote(source, target, send, recv, device):
        return pltpu.make_async_remote_copy(
            src_ref=source, dst_ref=target, send_sem=send, recv_sem=recv, device_id=device, device_id_type=mesh_id
        )

    peers = ((0, 1), (1, 0), (1, 1))
    far_q = pltpu.make_async_copy(q_far, q_raw, far_sem.at[0])
    far_g = pltpu.make_async_copy(g_far, g_raw, far_sem.at[1])
    far_q.start()
    far_g.start()

    barrier = pltpu.get_barrier_semaphore()
    for side, cross in peers:
        pl.semaphore_signal(barrier, inc=1, device_id=peer(side, cross), device_id_type=mesh_id)
    for other in range(outer):

        @pl.when(z != other)
        def _():
            pl.semaphore_signal(barrier, inc=1, device_id=level(other), device_id_type=mesh_id)

    def angles(side, depth_of):
        first = base_ref[depth_of]
        cosine, sine = first[0:1], first[1:2]
        cos_ref[side] = token_ref[0] * cosine - token_ref[1] * sine
        sin_ref[side] = token_ref[1] * cosine + token_ref[0] * sine

    depth_here = place_ref[0] // BLOCK
    angles(0, depth_here)
    for entry in range(width):
        note[0, entry] = list_ref[0, entry]
    note[0, width] = depth_here

    def turn(x, place, sign):
        cosine, sine = cos_ref[0, place, :], sin_ref[0, place, :]
        swapped = pltpu.roll(x, half, x.ndim - 1)
        return x * cosine[None] + swapped * (sign * sine)[None]

    def bring(raw, write, rotate):
        for start in range(0, tokens, step_tokens):
            x = jnp.transpose(raw[start : start + step_tokens].astype(f32), (1, 0, 2))
            if rotate:
                place = pl.ds(pl.multiple_of(core * tokens + start, step_tokens), step_tokens)
                x = turn(x, place, 1.0)
            write(slice(start, start + step_tokens), x.astype(low))

    def take(read, raw):
        for start in range(0, tokens, step_tokens):
            x = read(slice(start, start + step_tokens)).astype(f32)
            raw[start : start + step_tokens] = jnp.transpose(x, (1, 0, 2)).astype(low)

    def write_to(ref, lane=None):
        def write(place, x):
            if lane is None:
                ref[:, place, :] = x
            else:
                ref[:, lane, place, :] = x

        return write

    def send_note():
        return remote(note.at[0], note.at[1], note_send, note_recv, peer(1, 0))

    def swap_kv(h, r):
        return remote(
            kv_in.at[quarter_of(*peers[r]) * local + h], kv[h].at[me, :, mine, :], kv_send.at[h, r], kv_recv.at[h, r], peer(*peers[r])
        )

    def swap_q(h, r):
        source = pl.ds(quarter_of(*peers[r]) * heads + h * group, group)
        target = q_full.at[peers[r][0], pl.ds(h * group, group), mine, :]
        return remote(q_in.at[source], target, q_send.at[h, r], q_recv.at[h, r], peer(*peers[r]))

    def swap_g(h, r):
        source = pl.ds(quarter_of(*peers[r]) * heads + h * group, group)
        target = g_full.at[peers[r][0], pl.ds(h * group, group), mine, :]
        return remote(g_in.at[source], target, g_send.at[h, r], g_recv.at[h, r], peer(*peers[r]))

    def gather_z(h, side, far):
        view = kv[h].at[2 * z + row_of(side)]
        return remote(view, view, gz_send.at[h, side, far], gz_recv.at[h, side, z], level(far))

    def arrived_z(h, side, near):
        view = kv[h].at[2 * near + row_of(side)]
        return remote(view, view, gz_send.at[h, side, near], gz_recv.at[h, side, near], level(near))

    def reduce_z(h, side, near):
        return remote(
            z_send.at[h, near, side], z_part.at[h, z, side], rz_send.at[h, side, near], rz_recv.at[h, side, z], level(near)
        )

    def returned_z(h, side, far):
        return remote(
            z_send.at[h, far, side], z_part.at[h, far, side], rz_send.at[h, side, far], rz_recv.at[h, side, far], level(far)
        )

    def upward(h, side):
        for far in reversed(range(1, outer)):

            @pl.when(z < far)
            def _():
                gather_z(h, side, far).start()

    bring(k_raw, write_to(kv_in, 0), True)
    bring(v_raw, write_to(kv_in, 1), False)
    pl.semaphore_wait(barrier, outer + 2)
    for h in range(local):
        for r in range(3):
            swap_kv(h, r).start()
    send_note().start()
    for h in range(local):
        kv[h][me, :, mine, :] = kv_in[quarter * local + h]
    swap_kv(0, 0).wait_recv()
    upward(0, 0)
    far_q.wait()
    bring(q_raw, write_to(q_in), True)
    for r in range(3):
        swap_q(0, r).start()
    for r in (1, 2):
        swap_kv(0, r).wait_recv()
    upward(0, 1)
    swap_kv(1, 0).wait_recv()
    upward(1, 0)
    for r in (1, 2):
        swap_kv(1, r).wait_recv()
    upward(1, 1)
    far_g.wait()
    bring(g_raw, write_to(g_in), False)
    for r in range(3):
        swap_g(0, r).start()
    for h in range(1, local):
        for r in range(3):
            swap_q(h, r).start()
            swap_g(h, r).start()
    q_full[0, :, mine, :] = q_in[pl.ds(quarter * heads, heads)]
    g_full[0, :, mine, :] = g_in[pl.ds(quarter * heads, heads)]
    for side in range(2):
        part[side, width] = jnp.zeros(part.shape[2:], part.dtype)
    send_note().wait_recv()
    angles(1, note[1, width])

    def homeward(h, side):
        copies = []
        for r in range(3):
            if peers[r][0] != side:
                continue
            place = mine if peers[r][1] == 0 else theirs
            source = pl.ds(h * group, group)
            target = pl.ds(quarter * heads + h * group, group)
            copies.append(
                remote(out_full.at[side, source, place, :], out_home.at[target], out_send.at[h, r], out_recv.at[h, r], peer(*peers[r]))
            )
            copies.append(
                remote(qg_full.at[side, source, place, :], qg_home.at[target], qg_send.at[h, r], qg_recv.at[h, r], peer(*peers[r]))
            )
        return copies

    def attend(h, side):
        if side == 0:
            for near in range(outer - 1):
                for lane in range(2):

                    @pl.when(near < z)
                    def _():
                        arrived_z(h, lane, near).wait_recv()

            for r in range(3):
                swap_q(h, r).wait_recv()
                swap_g(h, r).wait_recv()
        block_here = 2 * z + row_of(side)
        first = h * group
        for entry in range(width):
            block = jnp.maximum(note[side, entry], 0)
            k_all[pl.ds(entry * BLOCK, BLOCK), :] = kv[h][block, 0]
            v_all[pl.ds(entry * BLOCK, BLOCK), :] = kv[h][block, 1]
        q = q_full[side, pl.ds(first, group)].reshape(rows, depth)
        g = g_full[side, pl.ds(first, group)].reshape(rows, depth)
        kk, vv = k_all[...], v_all[...]
        score = lax.dot_general(kk, q, nt, preferred_element_type=f32) * scale
        prob_grad = lax.dot_general(vv, g, nt, preferred_element_type=f32)
        key_row = lax.broadcasted_iota(jnp.int32, (BLOCK, rows), 0)
        query_row = lax.broadcasted_iota(jnp.int32, (BLOCK, rows), 1) % BLOCK
        causal = key_row <= query_row
        pieces = []
        for entry in range(width):
            block = note[side, entry]
            allowed = jnp.logical_and(block >= 0, jnp.logical_or(block != block_here, causal))
            pieces.append(jnp.where(allowed, score[entry * BLOCK : (entry + 1) * BLOCK], NEG_FILL))
        score = jnp.concatenate(pieces, axis=0)
        best = jnp.max(score, axis=0, keepdims=True)
        weights = jnp.exp(score - best)
        inverse = 1.0 / jnp.sum(weights, axis=0, keepdims=True)
        out_t = jnp.dot(vv.T, weights.astype(low), preferred_element_type=f32) * inverse
        out_low = out_t.astype(low)
        out_full[side, pl.ds(first, group)] = out_t.T.astype(low).reshape(group, BLOCK, depth)
        delta = jnp.sum(g.astype(f32).T * out_low.astype(f32), axis=0, keepdims=True)
        prob = weights * inverse
        score_grad = (prob * (prob_grad - delta)).astype(low)
        value_part = jnp.dot(prob.astype(low), g, preferred_element_type=f32).astype(low)
        key_part = (jnp.dot(score_grad, q, preferred_element_type=f32) * scale).astype(low)
        for entry in range(width):
            part[side, entry, 0] = key_part[entry * BLOCK : (entry + 1) * BLOCK]
            part[side, entry, 1] = value_part[entry * BLOCK : (entry + 1) * BLOCK]
        qg = (jnp.dot(kk.T, score_grad, preferred_element_type=f32) * scale).T
        qg = qg.reshape(group, BLOCK, depth)
        swapped = jnp.concatenate([qg[..., half:], qg[..., :half]], axis=-1)
        qg_full[side, pl.ds(first, group)] = (qg * cos_ref[side][None] - swapped * sin_ref[side][None]).astype(low)
        for copy in homeward(h, side):
            copy.start()
        if side == 0:
            target = pl.ds(quarter * heads + first, group)
            out_home[target] = out_full[0, pl.ds(first, group), mine, :]
            qg_home[target] = qg_full[0, pl.ds(first, group), mine, :]

    def slot_of(side, block):
        slot = jnp.int32(width)
        for entry in range(width):
            slot = jnp.where(note[side, entry] == block, entry, slot)
        return slot

    def spread(h):
        for near in range(outer):
            for lane in (1, 0):

                @pl.when(near <= z)
                def _():
                    block = 2 * near + row_of(lane)
                    total = part[0, slot_of(0, block)].astype(f32) + part[1, slot_of(1, block)].astype(f32)

                    @pl.when(near < z)
                    def _():
                        z_send[h, near, lane] = total.astype(low)
                        reduce_z(h, lane, near).start()

                    @pl.when(near == z)
                    def _():
                        own[h, lane] = total

    def kv_home(h, r):
        side, cross = peers[r]
        place = mine if cross == 0 else theirs
        return remote(
            kvg.at[h, side, :, place, :], kvg_home.at[quarter * local + h], home_send.at[h, r], home_recv.at[h, r], peer(side, cross)
        )

    def settle(h):
        for lane in (1, 0):
            acc[...] = own[h, lane]
            for far in range(1, outer):

                @pl.when(z < far)
                def _():
                    returned_z(h, lane, far).wait_recv()
                    acc[...] += z_part[h, far, lane].astype(f32)

            key_total = acc[0]
            swapped = jnp.concatenate([key_total[..., half:], key_total[..., :half]], axis=-1)
            kvg[h, lane, 0] = (key_total * cos_ref[lane] - swapped * sin_ref[lane]).astype(low)
            kvg[h, lane, 1] = acc[1].astype(low)
            for r in range(3):
                if peers[r][0] == lane:
                    kv_home(h, r).start()
        kvg_home[quarter * local + h] = kvg[h, 0, :, mine, :]

    for h in range(local):
        attend(h, 0)
        attend(h, 1)
        spread(h)
    for h in range(local - 1):
        settle(h)
    for h in range(local):
        for side in range(2):
            for copy in homeward(h, side):
                copy.wait()
    take(lambda place: out_home[:, place, :], out_raw)
    take(lambda place: qg_home[:, place, :], qg_raw)
    settle(local - 1)

    send_note().wait_send()
    for h in range(local):
        for r in range(3):
            swap_kv(h, r).wait_send()
            swap_q(h, r).wait_send()
            swap_g(h, r).wait_send()
        for side in range(2):
            for far in range(1, outer):

                @pl.when(z < far)
                def _():
                    gather_z(h, side, far).wait_send()

            for near in range(outer - 1):

                @pl.when(near < z)
                def _():
                    reduce_z(h, side, near).wait_send()

    for h in range(local):
        for r in range(3):
            kv_home(h, r).wait()
    take(lambda place: kvg_home[:, 0, place, :], kg_raw)
    take(lambda place: kvg_home[:, 1, place, :], vg_raw)


def angle_tables(width, depth):
    half = depth // 2
    frequency = ROPE_BASE ** (-2.0 * np.arange(half) / depth)

    def pair(place):
        angle = place[:, None] * frequency[None, :]
        cosine, sine = np.cos(angle), np.sin(angle)
        return np.stack([np.concatenate([cosine, cosine], -1), np.concatenate([-sine, sine], -1)]).astype(np.float32)

    token = pair(np.arange(BLOCK, dtype=np.float64))
    base = pair(np.arange(width, dtype=np.float64) * BLOCK)
    return token, np.moveaxis(base, 0, 1)


def quad(blocks, list_rows, places, q, k, v, g):
    tokens, heads, depth = q.shape
    key_heads = k.shape[1]
    group = heads // key_heads
    local = key_heads // 4
    width = list_rows.shape[1]
    outer = blocks // 2
    low, f32 = jnp.bfloat16, jnp.float32
    vmem, dma = pltpu.VMEM, pltpu.SemaphoreType.DMA
    whole = pl.BlockSpec(memory_space=pltpu.VMEM)
    scalar = pl.BlockSpec(memory_space=pltpu.SMEM)
    distant = pl.BlockSpec(memory_space=pl.ANY)
    token, base = angle_tables(width, depth)
    tile = (2, BLOCK, depth)
    full = (2, local * group, BLOCK, depth)
    scratch = [vmem((blocks,) + tile, low)] * local
    scratch += [vmem(q.shape, low)] * 2
    scratch += [vmem((key_heads, 2, tokens, depth), low)] + [vmem((heads, tokens, depth), low)] * 2
    scratch += [vmem(full, low)] * 4 + [vmem((heads, tokens, depth), low)] * 2
    scratch += [vmem((local, 2) + tile, low), vmem((key_heads, 2, tokens, depth), low)]
    scratch += [vmem((width * BLOCK, depth), low)] * 2
    scratch += [vmem((2, width + 1) + tile, low), vmem((local, 2) + tile, f32)]
    scratch += [vmem((local, outer, 2) + tile, low)] * 2
    scratch += [vmem(tile, f32)] + [vmem((2, BLOCK, depth), f32)] * 2
    scratch += [pltpu.SMEM((2, 2 * width), jnp.int32)]
    scratch += [dma((2,)), dma, dma] + [dma((local, 3))] * 12 + [dma((local, 2, outer))] * 4
    return pl.pallas_call(
        functools.partial(quad_kernel, outer, width, group, 1.0 / math.sqrt(depth)),
        in_specs=[scalar] * 2 + [whole] * 4 + [distant] * 2,
        out_specs=[whole] * 4,
        out_shape=[jax.ShapeDtypeStruct(x.shape, low) for x in (q, q, k, k)],
        scratch_shapes=scratch,
        compiler_params=pltpu.CompilerParams(
            collective_id=1, has_side_effects=True, vmem_limit_bytes=60 << 20
        ),
        name="quad_flow",
    )(list_rows, places, k, v, jnp.asarray(token), jnp.asarray(base), q, g)


def body(blocks, queries, keys, values, out_grad, block_list, positions):
    tokens, _, depth = queries.shape
    if blocks == 8:
        return tuple(quad(blocks, block_list, positions, queries, keys, values, out_grad))
    base = positions[0] - lax.axis_index("head") * tokens
    cosine, sine = tables(base + jnp.arange(BLOCK, dtype=jnp.int32), depth)
    return tuple(flow(blocks, block_list[0], queries, keys, values, out_grad, cosine, sine))


def solution(mesh):
    spec = P(("groups", "blk", "head"), None, None)
    in_specs = (spec, spec, spec, spec, P(("groups", "blk"), None), P(("groups", "blk", "head")))
    run = functools.partial(body, mesh.shape["blk"])
    return jax.shard_map(run, mesh=mesh, in_specs=in_specs, out_specs=(spec,) * 4, check_vma=False)
```

```python
import functools
import math

import jax
import jax.numpy as jnp
import numpy as np
from jax import lax
from jax.experimental import pallas as pl
from jax.experimental.pallas import tpu as pltpu
from jax.sharding import PartitionSpec as P

BLOCK = 128
ROPE_BASE = 10000.0
NEG_FILL = -1e30
LAG = 4
SKEW = 4
EARLY = ()


def tables(place, width):
    half = width // 2
    exponent = 2.0 * jnp.arange(half, dtype=jnp.float32) / width
    frequency = ROPE_BASE ** (-exponent)
    angle = place.astype(jnp.float32)[:, None] * frequency[None, :]
    cosine, sine = jnp.cos(angle), jnp.sin(angle)
    return jnp.concatenate([cosine, cosine], -1), jnp.concatenate([-sine, sine], -1)


def flow_kernel(
    blocks, inner, width, group, scale,
    list_ref, q_raw, k_raw, v_raw, g_raw, cos_ref, sin_ref, out_raw, qg_raw, kg_raw, vg_raw, *scratch,
):
    tokens, heads, depth = q_raw.shape
    heads = heads // 2
    key_heads = k_raw.shape[1] // 2
    outer = blocks // inner
    rows = group * BLOCK
    f32, low = jnp.float32, jnp.bfloat16
    nt = (((1,), (1,)), ((), ()))
    kv = scratch[:key_heads]
    (q_in, g_in, kv_in, out_home, qg_home, kvg_home, q_full, g_full, out_full, qg_full, kvg, k_all, v_all, part, own, y_send, y_part, z_send, z_part, acc, total_kv,
     core_send, core_recv, gz_send, gz_recv, gy_send, gy_recv, ry_send, ry_recv, rz_send, rz_recv) = scratch[key_heads:]

    me = lax.axis_index("blk")
    core = lax.axis_index("head")
    other = 1 - core
    z, y = me // inner, me % inner
    up, down = {"blk": me + inner}, {"blk": me - inner}
    side = {"blk": z * inner + (inner - 1 - y)}
    twin = {"head": other}
    mesh_id = pl.DeviceIdType.MESH
    mine = pl.ds(pl.multiple_of(core * tokens, tokens), tokens)
    theirs = pl.ds(pl.multiple_of(other * tokens, tokens), tokens)

    def remote(source, target, send, recv, device):
        return pltpu.make_async_remote_copy(
            src_ref=source, dst_ref=target, send_sem=send, recv_sem=recv, device_id=device, device_id_type=mesh_id
        )

    def repeat(count, step):
        if count <= 4:
            for index in range(count):
                step(index)
        else:
            lax.fori_loop(0, count, lambda index, carry: (step(index), carry)[1], 0)

    barrier = pltpu.get_barrier_semaphore()
    pl.semaphore_signal(barrier, inc=1, device_id=twin, device_id_type=mesh_id)
    if inner > 1:
        pl.semaphore_signal(barrier, inc=1, device_id=side, device_id_type=mesh_id)

    @pl.when(z > 0)
    def _():
        pl.semaphore_signal(barrier, inc=1, device_id=down, device_id_type=mesh_id)

    @pl.when(z < outer - 1)
    def _():
        pl.semaphore_signal(barrier, inc=1, device_id=up, device_id_type=mesh_id)

    peers = (2 if inner > 1 else 1) + (z + outer - 1) // outer + (2 * outer - 2 - z) // outer
    pl.semaphore_wait(barrier, peers)

    half = depth // 2
    step_tokens = 16

    def turn(x, place, sign):
        cosine, sine = cos_ref[place, :], sin_ref[place, :]
        swapped = pltpu.roll(x, half, x.ndim - 1)
        return x * cosine[None] + swapped * (sign * sine)[None]

    def bring(raw, write, rotate):
        for start in range(0, tokens, step_tokens):
            x = jnp.transpose(raw[start : start + step_tokens].astype(f32), (1, 0, 2))
            if rotate:
                place = pl.ds(pl.multiple_of(core * tokens + start, step_tokens), step_tokens)
                x = turn(x, place, 1.0)
            write(slice(start, start + step_tokens), x.astype(low))

    def take(read, raw):
        for start in range(0, tokens, step_tokens):
            x = read(slice(start, start + step_tokens)).astype(f32)
            raw[start : start + step_tokens] = jnp.transpose(x, (1, 0, 2)).astype(low)

    def write_to(ref, lane=None):
        def write(place, x):
            if lane is None:
                ref[:, place, :] = x
            else:
                ref[:, lane, place, :] = x

        return write

    bring(k_raw, write_to(kv_in, 0), True)
    bring(v_raw, write_to(kv_in, 1), False)
    swaps = []
    for h in range(key_heads):
        swaps.append(
            remote(kv_in.at[other * key_heads + h], kv[h].at[me, :, mine, :], core_send.at[h], core_recv.at[h], twin)
        )
    k = key_heads
    swaps.append(
        remote(q_in.at[pl.ds(other * heads, heads)], q_full.at[:, mine, :], core_send.at[k], core_recv.at[k], twin)
    )
    swaps.append(
        remote(g_in.at[pl.ds(other * heads, heads)], g_full.at[:, mine, :], core_send.at[k + 1], core_recv.at[k + 1], twin)
    )
    for copy in swaps[:key_heads]:
        copy.start()
    for h in range(key_heads):
        kv[h][me, :, mine, :] = kv_in[core * key_heads + h]

    def bring_queries():
        bring(q_raw, write_to(q_in), True)
        swaps[key_heads].start()
        bring(g_raw, write_to(g_in), False)
        swaps[key_heads + 1].start()
        q_full[:, mine, :] = q_in[pl.ds(core * heads, heads)]
        g_full[:, mine, :] = g_in[pl.ds(core * heads, heads)]
        part[width] = jnp.zeros(part.shape[1:], part.dtype)

    def early(h):
        return inner > 1 and h in EARLY

    def lanes(h):
        return 2 if early(h) else 1

    def column(lane):
        return y if lane == 0 else inner - 1 - y

    def gather_z(s, h, lane):
        view = kv[h].at[(z - s) * inner + column(lane)]
        return remote(view, view, gz_send.at[s, h, lane], gz_recv.at[s, h, lane], up)

    def arrived_z(s, h, lane):
        view = kv[h].at[(z - s) * inner + column(lane)]
        return remote(view, view, gz_send.at[s - 1, h, lane], gz_recv.at[s - 1, h, lane], down)

    def gather_y(s, h):
        view = kv[h].at[(z - s) * inner + column(0)]
        return remote(view, view, gy_send.at[s, h], gy_recv.at[s, h], side)

    def arrived_y(s, h):
        view = kv[h].at[(z - s) * inner + column(1)]
        return remote(view, view, gy_send.at[s, h], gy_recv.at[s, h], side)

    def crosses(s, h):
        return inner > 1 and (s == 0 or not early(h))

    def sends_y(s, h):
        return (z >= s) & (y == 0) if s == 0 and not early(h) else z >= s

    def takes_y(s, h):
        return (z >= s) & (y == 1) if s == 0 and not early(h) else z >= s

    def forward(s, h):
        if s == 0:
            swaps[h].wait_recv()
            if early(h):
                gather_y(0, h).start()
        for lane in range(lanes(h)):
            if s > 0:

                @pl.when(z >= s)
                def _():
                    arrived_z(s, h, lane).wait_recv()

            elif lane == 1:
                arrived_y(0, h).wait_recv()

            @pl.when((z >= s) & (z < outer - 1))
            def _():
                gather_z(s, h, lane).start()

        if crosses(s, h) and not early(h):

            @pl.when(sends_y(s, h))
            def _():
                gather_y(s, h).start()

    def attend(h):
        if inner > 1 and not early(h):
            for s in range(outer):

                @pl.when(takes_y(s, h))
                def _():
                    arrived_y(s, h).wait_recv()

        if h == 0:
            swaps[key_heads].wait_recv()
            swaps[key_heads + 1].wait_recv()
        first = h * group
        for entry in range(width):
            block = jnp.maximum(list_ref[entry], 0)
            k_all[pl.ds(entry * BLOCK, BLOCK), :] = kv[h][block, 0]
            v_all[pl.ds(entry * BLOCK, BLOCK), :] = kv[h][block, 1]
        q = q_full[pl.ds(first, group)].reshape(rows, depth)
        g = g_full[pl.ds(first, group)].reshape(rows, depth)
        kk, vv = k_all[...], v_all[...]
        score = lax.dot_general(kk, q, nt, preferred_element_type=f32) * scale
        prob_grad = lax.dot_general(vv, g, nt, preferred_element_type=f32)
        key_row = lax.broadcasted_iota(jnp.int32, (BLOCK, rows), 0)
        query_row = lax.broadcasted_iota(jnp.int32, (BLOCK, rows), 1) % BLOCK
        causal = key_row <= query_row
        pieces = []
        for entry in range(width):
            block = list_ref[entry]
            allowed = jnp.logical_and(block >= 0, jnp.logical_or(block != me, causal))
            pieces.append(jnp.where(allowed, score[entry * BLOCK : (entry + 1) * BLOCK], NEG_FILL))
        score = jnp.concatenate(pieces, axis=0)
        best = jnp.max(score, axis=0, keepdims=True)
        weights = jnp.exp(score - best)
        inverse = 1.0 / jnp.sum(weights, axis=0, keepdims=True)
        out_t = jnp.dot(vv.T, weights.astype(low), preferred_element_type=f32) * inverse
        out_low = out_t.astype(low)
        out_full[pl.ds(first, group)] = out_t.T.astype(low).reshape(group, BLOCK, depth)
        delta = jnp.sum(g.astype(f32).T * out_low.astype(f32), axis=0, keepdims=True)
        prob = weights * inverse
        score_grad = (prob * (prob_grad - delta)).astype(low)
        value_part = jnp.dot(prob.astype(low), g, preferred_element_type=f32).astype(low)
        key_part = (jnp.dot(score_grad, q, preferred_element_type=f32) * scale).astype(low)
        for entry in range(width):
            part[entry, 0] = key_part[entry * BLOCK : (entry + 1) * BLOCK]
            part[entry, 1] = value_part[entry * BLOCK : (entry + 1) * BLOCK]

        def place(block):
            slot = jnp.int32(width)
            for entry in range(width):
                slot = jnp.where(list_ref[entry] == block, entry, slot)
            return slot

        def spread(zd):
            if inner > 1 and not early(h):

                @pl.when((zd < z) | ((zd == z) & (y == 1)))
                def _():
                    y_send[h, zd] = part[place(zd * inner + column(1))]
                    reduce_y(zd, h).start()

            for lane in range(lanes(h)):
                own[h, zd, lane] = part[place(zd * inner + column(lane))]

        repeat(outer, spread)
        qg = (jnp.dot(kk.T, score_grad, preferred_element_type=f32) * scale).T
        qg = qg.reshape(group, BLOCK, depth)
        half = depth // 2
        swapped = jnp.concatenate([qg[..., half:], qg[..., :half]], axis=-1)
        qg_full[pl.ds(first, group)] = (qg * cos_ref[...][None] - swapped * sin_ref[...][None]).astype(low)
        for copy in homeward(h):
            copy.start()
        out_home[pl.ds(core * heads + first, group)] = out_full[pl.ds(first, group), mine, :]
        qg_home[pl.ds(core * heads + first, group)] = qg_full[pl.ds(first, group), mine, :]

    def homeward(h):
        source, target = pl.ds(h * group, group), pl.ds(core * heads + h * group, group)
        a, b = key_heads + 2 + h, 2 * key_heads + 2 + h
        return (
            remote(out_full.at[source, theirs, :], out_home.at[target], core_send.at[a], core_recv.at[a], twin),
            remote(qg_full.at[source, theirs, :], qg_home.at[target], core_send.at[b], core_recv.at[b], twin),
        )

    def reduce_y(zd, h):
        return remote(y_send.at[h, zd], y_part.at[h, zd], ry_send.at[zd, h], ry_recv.at[zd, h], side)

    def reduce_z(zd, h, lane):
        return remote(
            z_send.at[h, zd, lane], z_part.at[h, zd, lane], rz_send.at[zd, h, lane], rz_recv.at[zd, h, lane], down
        )

    def reduce(h):
        def one(zd):
            for lane in reversed(range(lanes(h))):

                @pl.when(zd <= z)
                def _():
                    acc[...] = own[h, zd, lane].astype(f32)

                    if inner > 1 and not early(h):

                        @pl.when((zd < z) | (y == 0))
                        def _():
                            reduce_y(zd, h).wait_recv()
                            acc[...] += y_part[h, zd].astype(f32)

                    @pl.when(z < outer - 1)
                    def _():
                        reduce_z(zd, h, lane).wait_recv()
                        acc[...] += z_part[h, zd, lane].astype(f32)

                    @pl.when(zd < z)
                    def _():
                        z_send[h, zd, lane] = acc[...].astype(low)
                        reduce_z(zd, h, lane).start()

                    @pl.when(zd == z)
                    def _():
                        if lane == 1:
                            y_send[h, zd] = acc[...].astype(low)
                            reduce_y(zd, h).start()
                        else:
                            total_kv[h] = acc[...]

        repeat(outer, one)

    def settle(h):
        if early(h):
            reduce_y(z, h).wait_recv()
            total_kv[h] += y_part[h, z].astype(f32)

    moves = sorted((h + SKEW * s, s, h) for h in range(key_heads) for s in range(outer))
    ends = [moves.index((h + SKEW * (outer - 1), outer - 1, h)) for h in range(key_heads)]
    ready = [min(end + LAG, len(moves) - 1) for end in ends]
    for step, (_, s, h) in enumerate(moves):
        forward(s, h)
        if step == key_heads - 1:
            bring_queries()
        for done in range(key_heads):
            if ready[done] == step:
                attend(done)
                if done >= 1:
                    reduce(done - 1)
    for h in range(key_heads):
        for copy in homeward(h):
            copy.wait()
    take(lambda place: out_home[:, place, :], out_raw)
    take(lambda place: qg_home[:, place, :], qg_raw)
    reduce(key_heads - 1)
    for h in range(key_heads):
        settle(h)

    key_total = total_kv[:, 0]
    half = depth // 2
    swapped = jnp.concatenate([key_total[..., half:], key_total[..., :half]], axis=-1)
    kvg[:, 0] = (key_total * cos_ref[...][None] - swapped * sin_ref[...][None]).astype(low)
    kvg[:, 1] = total_kv[:, 1].astype(low)
    final = 3 * key_heads + 2
    target = pl.ds(core * key_heads, key_heads)
    closing = remote(kvg.at[:, :, theirs, :], kvg_home.at[target], core_send.at[final], core_recv.at[final], twin)
    closing.start()
    kvg_home[target] = kvg[:, :, mine, :]

    for copy in swaps:
        copy.wait_send()
    for h in range(key_heads):
        for s in range(outer):

            for lane in range(lanes(h)):

                @pl.when((z >= s) & (z < outer - 1))
                def _():
                    gather_z(s, h, lane).wait_send()

                @pl.when(s < z)
                def _():
                    reduce_z(s, h, lane).wait_send()

            if crosses(s, h):

                @pl.when(sends_y(s, h))
                def _():
                    gather_y(s, h).wait_send()

            if inner > 1 and not early(h):

                @pl.when((s < z) | ((s == z) & (y == 1)))
                def _():
                    reduce_y(s, h).wait_send()

        if early(h):
            reduce_y(z, h).wait_send()
    closing.wait()
    take(lambda place: kvg_home[:, 0, place, :], kg_raw)
    take(lambda place: kvg_home[:, 1, place, :], vg_raw)


def flow(blocks, list_row, q, k, v, g, cosine, sine):
    tokens, heads, depth = q.shape
    key_heads = k.shape[1] // 2
    group = heads // k.shape[1]
    width = list_row.shape[0]
    inner = 2 if blocks == 8 else 1
    outer = blocks // inner
    low, f32 = jnp.bfloat16, jnp.float32
    vmem, dma = pltpu.VMEM, pltpu.SemaphoreType.DMA
    whole = pl.BlockSpec(memory_space=pltpu.VMEM)
    half_heads = (heads // 2, BLOCK, depth)
    tile = (2, BLOCK, depth)
    sided = (key_heads, outer if inner > 1 else 1) + tile
    flags = (outer, key_heads)
    scratch = [vmem((blocks,) + tile, low)] * key_heads
    home = [vmem((heads, tokens, depth), low)] * 2 + [vmem((2 * key_heads, 2, tokens, depth), low)]
    scratch += home + home + [vmem(half_heads, low)] * 4
    scratch += [vmem((key_heads,) + tile, low)]
    scratch += [vmem((width * BLOCK, depth), low)] * 2
    scratch += [vmem((width + 1,) + tile, low)]
    scratch += [vmem((key_heads, outer, inner) + tile, low)]
    scratch += [vmem(sided, low)] * 2
    scratch += [vmem((key_heads, outer, inner) + tile, low)] * 2
    scratch += [vmem(tile, f32), vmem((key_heads,) + tile, f32)]
    scratch += [dma((3 * key_heads + 3,))] * 2
    scratch += [dma(flags + (inner,))] * 2 + [dma(flags)] * 4 + [dma(flags + (inner,))] * 2
    return pl.pallas_call(
        functools.partial(flow_kernel, blocks, inner, width, group, 1.0 / math.sqrt(depth)),
        in_specs=[pl.BlockSpec(memory_space=pltpu.SMEM)] + [whole] * 6,
        out_specs=[whole] * 4,
        out_shape=[jax.ShapeDtypeStruct(x.shape, low) for x in (q, q, k, k)],
        scratch_shapes=scratch,
        compiler_params=pltpu.CompilerParams(
            collective_id=0, has_side_effects=True, vmem_limit_bytes=60 << 20
        ),
        name="flow",
    )(list_row, q, k, v, g, cosine, sine)


def quad_kernel(
    outer, width, group, scale,
    list_ref, place_ref, k_raw, v_raw, token_ref, base_ref, q_far, g_far, out_raw, qg_raw, kg_raw, vg_raw, *scratch,
):
    tokens, key_heads, depth = k_raw.shape
    local = key_heads // 4
    heads = local * group
    rows = group * BLOCK
    f32, low = jnp.float32, jnp.bfloat16
    nt = (((1,), (1,)), ((), ()))
    kv = scratch[:local]
    (q_raw, g_raw, kv_in, q_in, g_in, q_full, g_full, out_full, qg_full, out_home, qg_home, kvg, kvg_home, k_all, v_all, part,
     own, z_send, z_part, acc, cos_ref, sin_ref, note,
     far_sem, note_send, note_recv, kv_send, kv_recv, q_send, q_recv, g_send, g_recv, out_send, out_recv, qg_send, qg_recv,
     home_send, home_recv, gz_send, gz_recv, rz_send, rz_recv, relay_recv, relay, pending) = scratch[local:]

    me = lax.axis_index("blk")
    core = lax.axis_index("head")
    z, y = me // 2, me % 2
    quarter = 2 * y + core
    mesh_id = pl.DeviceIdType.MESH
    mine = pl.ds(pl.multiple_of(core * tokens, tokens), tokens)
    theirs = pl.ds(pl.multiple_of((1 - core) * tokens, tokens), tokens)
    half = depth // 2
    step_tokens = 16

    def row_of(side):
        return y if side == 0 else 1 - y

    def core_of(cross):
        return core if cross == 0 else 1 - core

    def peer(side, cross):
        return {"blk": 2 * z + row_of(side), "head": core_of(cross)}

    def quarter_of(side, cross):
        return 2 * row_of(side) + core_of(cross)

    def level(other):
        return {"blk": 2 * other + y}

    def remote(source, target, send, recv, device):
        return pltpu.make_async_remote_copy(
            src_ref=source, dst_ref=target, send_sem=send, recv_sem=recv, device_id=device, device_id_type=mesh_id
        )

    peers = ((0, 1), (1, 0), (1, 1))
    far_q = pltpu.make_async_copy(q_far, q_raw, far_sem.at[0])
    far_g = pltpu.make_async_copy(g_far, g_raw, far_sem.at[1])
    far_q.start()
    far_g.start()

    barrier = pltpu.get_barrier_semaphore()
    for side, cross in peers:
        pl.semaphore_signal(barrier, inc=1, device_id=peer(side, cross), device_id_type=mesh_id)
    for other in range(outer):

        @pl.when(z != other)
        def _():
            pl.semaphore_signal(barrier, inc=1, device_id=level(other), device_id_type=mesh_id)

    def angles(side, depth_of):
        first = base_ref[depth_of]
        cosine, sine = first[0:1], first[1:2]
        cos_ref[side] = token_ref[0] * cosine - token_ref[1] * sine
        sin_ref[side] = token_ref[1] * cosine + token_ref[0] * sine

    depth_here = place_ref[0] // BLOCK
    angles(0, depth_here)
    for entry in range(width):
        note[0, entry] = list_ref[0, entry]
    note[0, width] = depth_here

    def turn(x, place, sign):
        cosine, sine = cos_ref[0, place, :], sin_ref[0, place, :]
        swapped = pltpu.roll(x, half, x.ndim - 1)
        return x * cosine[None] + swapped * (sign * sine)[None]

    def bring(raw, write, rotate):
        for start in range(0, tokens, step_tokens):
            x = jnp.transpose(raw[start : start + step_tokens].astype(f32), (1, 0, 2))
            if rotate:
                place = pl.ds(pl.multiple_of(core * tokens + start, step_tokens), step_tokens)
                x = turn(x, place, 1.0)
            write(slice(start, start + step_tokens), x.astype(low))

    def take(read, raw):
        for start in range(0, tokens, step_tokens):
            x = read(slice(start, start + step_tokens)).astype(f32)
            raw[start : start + step_tokens] = jnp.transpose(x, (1, 0, 2)).astype(low)

    def write_to(ref, lane=None):
        def write(place, x):
            if lane is None:
                ref[:, place, :] = x
            else:
                ref[:, lane, place, :] = x

        return write

    def send_note():
        return remote(note.at[0], note.at[1], note_send, note_recv, peer(1, 0))

    def swap_kv(h, r):
        return remote(
            kv_in.at[quarter_of(*peers[r]) * local + h], kv[h].at[me, :, mine, :], kv_send.at[h, r], kv_recv.at[h, r], peer(*peers[r])
        )

    def swap_q(h, r):
        source = pl.ds(quarter_of(*peers[r]) * heads + h * group, group)
        target = q_full.at[peers[r][0], pl.ds(h * group, group), mine, :]
        return remote(q_in.at[source], target, q_send.at[h, r], q_recv.at[h, r], peer(*peers[r]))

    def swap_g(h, r):
        source = pl.ds(quarter_of(*peers[r]) * heads + h * group, group)
        target = g_full.at[peers[r][0], pl.ds(h * group, group), mine, :]
        return remote(g_in.at[source], target, g_send.at[h, r], g_recv.at[h, r], peer(*peers[r]))

    def gather_z(h, side, far):
        view = kv[h].at[2 * z + row_of(side)]
        return remote(view, view, gz_send.at[h, side, far], gz_recv.at[h, side, z], level(far))

    def arrived_z(h, side, near):
        view = kv[h].at[2 * near + row_of(side)]
        return remote(view, view, gz_send.at[h, side, near], gz_recv.at[h, side, near], level(near))

    def reduce_z(h, side, near):
        return remote(
            z_send.at[h, near, side], z_part.at[h, z, side], rz_send.at[h, side, near], rz_recv.at[h, side, z], level(near)
        )

    def returned_z(h, side, far):
        return remote(
            z_send.at[h, far, side], z_part.at[h, far, side], rz_send.at[h, side, far], rz_recv.at[h, side, far], level(far)
        )

    last, relay_level = outer - 1, outer - 2

    def upward(h, side):
        for far in reversed(range(1, outer)):

            @pl.when((z < far) & (far - z < last))
            def _():
                gather_z(h, side, far).start()

    def relayed_up(h, side):
        view = kv[h].at[row_of(side)]
        return remote(view, view, gz_send.at[h, side, 0], gz_recv.at[h, side, 0], level(last))

    def pass_up(h, side):
        @pl.when(z == relay_level)
        def _():
            arrived_z(h, side, 0).wait_recv()
            relayed_up(h, side).start()

    def relayed_down(h, side):
        return remote(
            z_send.at[h, 0, side], relay.at[h, side], rz_send.at[h, side, 0], relay_recv.at[h, side], level(relay_level)
        )

    def pass_down(h):
        for lane in (1, 0):

            @pl.when(z == relay_level)
            def _():
                relayed_down(h, lane).wait_recv()
                z_send[h, 0, lane] = (pending[h, lane] + relay[h, lane].astype(f32)).astype(low)
                reduce_z(h, lane, 0).start()

    bring(k_raw, write_to(kv_in, 0), True)
    bring(v_raw, write_to(kv_in, 1), False)
    pl.semaphore_wait(barrier, outer + 2)
    for h in range(local):
        for r in range(3):
            swap_kv(h, r).start()
    send_note().start()
    for h in range(local):
        kv[h][me, :, mine, :] = kv_in[quarter * local + h]
    swap_kv(0, 0).wait_recv()
    upward(0, 0)
    far_q.wait()
    bring(q_raw, write_to(q_in), True)
    for r in range(3):
        swap_q(0, r).start()
    for r in (1, 2):
        swap_kv(0, r).wait_recv()
    upward(0, 1)
    swap_kv(1, 0).wait_recv()
    upward(1, 0)
    for r in (1, 2):
        swap_kv(1, r).wait_recv()
    upward(1, 1)
    far_g.wait()
    bring(g_raw, write_to(g_in), False)
    for r in range(3):
        swap_g(0, r).start()
    for h in range(1, local):
        for r in range(3):
            swap_q(h, r).start()
            swap_g(h, r).start()
    q_full[0, :, mine, :] = q_in[pl.ds(quarter * heads, heads)]
    g_full[0, :, mine, :] = g_in[pl.ds(quarter * heads, heads)]
    for side in range(2):
        part[side, width] = jnp.zeros(part.shape[2:], part.dtype)
    send_note().wait_recv()
    angles(1, note[1, width])

    def homeward(h, side):
        copies = []
        for r in range(3):
            if peers[r][0] != side:
                continue
            place = mine if peers[r][1] == 0 else theirs
            source = pl.ds(h * group, group)
            target = pl.ds(quarter * heads + h * group, group)
            copies.append(
                remote(out_full.at[side, source, place, :], out_home.at[target], out_send.at[h, r], out_recv.at[h, r], peer(*peers[r]))
            )
            copies.append(
                remote(qg_full.at[side, source, place, :], qg_home.at[target], qg_send.at[h, r], qg_recv.at[h, r], peer(*peers[r]))
            )
        return copies

    def attend(h, side):
        if side == 1:
            for near in range(outer - 1):
                for lane in range(2):

                    @pl.when((near < z) & ((near > 0) | (z != relay_level)))
                    def _():
                        arrived_z(h, lane, near).wait_recv()

            for r in range(3):
                swap_q(h, r).wait_recv()
                swap_g(h, r).wait_recv()
        block_here = 2 * z + row_of(side)
        first = h * group
        for entry in range(width):
            block = jnp.maximum(note[side, entry], 0)
            k_all[pl.ds(entry * BLOCK, BLOCK), :] = kv[h][block, 0]
            v_all[pl.ds(entry * BLOCK, BLOCK), :] = kv[h][block, 1]
        q = q_full[side, pl.ds(first, group)].reshape(rows, depth)
        g = g_full[side, pl.ds(first, group)].reshape(rows, depth)
        kk, vv = k_all[...], v_all[...]
        score = lax.dot_general(kk, q, nt, preferred_element_type=f32) * scale
        prob_grad = lax.dot_general(vv, g, nt, preferred_element_type=f32)
        key_row = lax.broadcasted_iota(jnp.int32, (BLOCK, rows), 0)
        query_row = lax.broadcasted_iota(jnp.int32, (BLOCK, rows), 1) % BLOCK
        causal = key_row <= query_row
        pieces = []
        for entry in range(width):
            block = note[side, entry]
            allowed = jnp.logical_and(block >= 0, jnp.logical_or(block != block_here, causal))
            pieces.append(jnp.where(allowed, score[entry * BLOCK : (entry + 1) * BLOCK], NEG_FILL))
        score = jnp.concatenate(pieces, axis=0)
        best = jnp.max(score, axis=0, keepdims=True)
        weights = jnp.exp(score - best)
        inverse = 1.0 / jnp.sum(weights, axis=0, keepdims=True)
        out_t = jnp.dot(vv.T, weights.astype(low), preferred_element_type=f32) * inverse
        out_low = out_t.astype(low)
        out_full[side, pl.ds(first, group)] = out_t.T.astype(low).reshape(group, BLOCK, depth)
        delta = jnp.sum(g.astype(f32).T * out_low.astype(f32), axis=0, keepdims=True)
        prob = weights * inverse
        score_grad = (prob * (prob_grad - delta)).astype(low)
        value_part = jnp.dot(prob.astype(low), g, preferred_element_type=f32).astype(low)
        key_part = (jnp.dot(score_grad, q, preferred_element_type=f32) * scale).astype(low)
        for entry in range(width):
            part[side, entry, 0] = key_part[entry * BLOCK : (entry + 1) * BLOCK]
            part[side, entry, 1] = value_part[entry * BLOCK : (entry + 1) * BLOCK]
        qg = (jnp.dot(kk.T, score_grad, preferred_element_type=f32) * scale).T
        qg = qg.reshape(group, BLOCK, depth)
        swapped = jnp.concatenate([qg[..., half:], qg[..., :half]], axis=-1)
        qg_full[side, pl.ds(first, group)] = (qg * cos_ref[side][None] - swapped * sin_ref[side][None]).astype(low)
        for copy in homeward(h, side):
            copy.start()
        if side == 0:
            target = pl.ds(quarter * heads + first, group)
            out_home[target] = out_full[0, pl.ds(first, group), mine, :]
            qg_home[target] = qg_full[0, pl.ds(first, group), mine, :]

    def slot_of(side, block):
        slot = jnp.int32(width)
        for entry in range(width):
            slot = jnp.where(note[side, entry] == block, entry, slot)
        return slot

    def spread(h):
        for near in range(outer):
            for lane in (1, 0):

                @pl.when(near <= z)
                def _():
                    block = 2 * near + row_of(lane)
                    total = part[0, slot_of(0, block)].astype(f32) + part[1, slot_of(1, block)].astype(f32)

                    @pl.when((near < z) & ((near > 0) | (z < relay_level)))
                    def _():
                        z_send[h, near, lane] = total.astype(low)
                        reduce_z(h, lane, near).start()

                    if near == 0:

                        @pl.when(z == relay_level)
                        def _():
                            pending[h, lane] = total

                        @pl.when(z == last)
                        def _():
                            z_send[h, near, lane] = total.astype(low)
                            relayed_down(h, lane).start()

                    @pl.when(near == z)
                    def _():
                        own[h, lane] = total

    def kv_home(h, r):
        side, cross = peers[r]
        place = mine if cross == 0 else theirs
        return remote(
            kvg.at[h, side, :, place, :], kvg_home.at[quarter * local + h], home_send.at[h, r], home_recv.at[h, r], peer(side, cross)
        )

    def settle(h):
        for lane in (1, 0):
            acc[...] = own[h, lane]
            for far in range(1, outer):

                @pl.when((z < far) & (far - z < last))
                def _():
                    returned_z(h, lane, far).wait_recv()
                    acc[...] += z_part[h, far, lane].astype(f32)

            key_total = acc[0]
            swapped = jnp.concatenate([key_total[..., half:], key_total[..., :half]], axis=-1)
            kvg[h, lane, 0] = (key_total * cos_ref[lane] - swapped * sin_ref[lane]).astype(low)
            kvg[h, lane, 1] = acc[1].astype(low)
            for r in range(3):
                if peers[r][0] == lane:
                    kv_home(h, r).start()
        kvg_home[quarter * local + h] = kvg[h, 0, :, mine, :]

    pass_up(0, 0)
    pass_up(0, 1)
    for h in range(local):
        attend(h, 1)
        if h + 1 < local:
            pass_up(h + 1, 0)
        if h > 0:
            pass_down(h - 1)
        attend(h, 0)
        if h + 1 < local:
            pass_up(h + 1, 1)
        spread(h)
    pass_down(local - 1)
    for h in range(local - 1):
        settle(h)
    for h in range(local):
        for side in range(2):
            for copy in homeward(h, side):
                copy.wait()
    take(lambda place: out_home[:, place, :], out_raw)
    take(lambda place: qg_home[:, place, :], qg_raw)
    settle(local - 1)

    send_note().wait_send()
    for h in range(local):
        for r in range(3):
            swap_kv(h, r).wait_send()
            swap_q(h, r).wait_send()
            swap_g(h, r).wait_send()
        for side in range(2):
            for far in range(1, outer):

                @pl.when((z < far) & (far - z < last))
                def _():
                    gather_z(h, side, far).wait_send()

            @pl.when(z == relay_level)
            def _():
                relayed_up(h, side).wait_send()

            for near in range(outer - 1):

                @pl.when((near < z) & (z - near < last))
                def _():
                    reduce_z(h, side, near).wait_send()

            @pl.when(z == last)
            def _():
                relayed_down(h, side).wait_send()

    for h in range(local):
        for r in range(3):
            kv_home(h, r).wait()
    take(lambda place: kvg_home[:, 0, place, :], kg_raw)
    take(lambda place: kvg_home[:, 1, place, :], vg_raw)


def store_kernel(*refs):
    done = refs[8]
    copies = [pltpu.make_async_copy(refs[index], refs[4 + index], done.at[index]) for index in range(4)]
    for copy in copies:
        copy.start()
    for copy in copies:
        copy.wait()


def angle_tables(width, depth):
    half = depth // 2
    frequency = ROPE_BASE ** (-2.0 * np.arange(half) / depth)

    def pair(place):
        angle = place[:, None] * frequency[None, :]
        cosine, sine = np.cos(angle), np.sin(angle)
        return np.stack([np.concatenate([cosine, cosine], -1), np.concatenate([-sine, sine], -1)]).astype(np.float32)

    token = pair(np.arange(BLOCK, dtype=np.float64))
    base = pair(np.arange(width, dtype=np.float64) * BLOCK)
    return token, np.moveaxis(base, 0, 1)


def quad(blocks, list_rows, places, q, k, v, g):
    tokens, heads, depth = q.shape
    key_heads = k.shape[1]
    group = heads // key_heads
    local = key_heads // 4
    width = list_rows.shape[1]
    outer = blocks // 2
    low, f32 = jnp.bfloat16, jnp.float32
    vmem, dma = pltpu.VMEM, pltpu.SemaphoreType.DMA
    whole = pl.BlockSpec(memory_space=pltpu.VMEM)
    scalar = pl.BlockSpec(memory_space=pltpu.SMEM)
    distant = pl.BlockSpec(memory_space=pl.ANY)
    token, base = angle_tables(width, depth)
    tile = (2, BLOCK, depth)
    full = (2, local * group, BLOCK, depth)
    scratch = [vmem((blocks,) + tile, low)] * local
    scratch += [vmem(q.shape, low)] * 2
    scratch += [vmem((key_heads, 2, tokens, depth), low)] + [vmem((heads, tokens, depth), low)] * 2
    scratch += [vmem(full, low)] * 4 + [vmem((heads, tokens, depth), low)] * 2
    scratch += [vmem((local, 2) + tile, low), vmem((key_heads, 2, tokens, depth), low)]
    scratch += [vmem((width * BLOCK, depth), low)] * 2
    scratch += [vmem((2, width + 1) + tile, low), vmem((local, 2) + tile, f32)]
    scratch += [vmem((local, outer, 2) + tile, low)] * 2
    scratch += [vmem(tile, f32)] + [vmem((2, BLOCK, depth), f32)] * 2
    scratch += [pltpu.SMEM((2, 2 * width), jnp.int32)]
    scratch += [dma((2,)), dma, dma] + [dma((local, 3))] * 12 + [dma((local, 2, outer))] * 4
    scratch += [dma((local, 2)), vmem((local, 2) + tile, low), vmem((local, 2) + tile, f32)]
    results = pl.pallas_call(
        functools.partial(quad_kernel, outer, width, group, 1.0 / math.sqrt(depth)),
        in_specs=[scalar] * 2 + [whole] * 4 + [distant] * 2,
        out_specs=[whole] * 4,
        out_shape=[vmem(x.shape, low) for x in (q, q, k, k)],
        scratch_shapes=scratch,
        compiler_params=pltpu.CompilerParams(
            collective_id=1, has_side_effects=True, vmem_limit_bytes=60 << 20
        ),
        name="quad_flow",
    )(list_rows, places, k, v, jnp.asarray(token), jnp.asarray(base), q, g)
    return pl.pallas_call(
        store_kernel,
        in_specs=[distant] * 4,
        out_specs=[distant] * 4,
        out_shape=[jax.ShapeDtypeStruct(x.shape, low) for x in (q, q, k, k)],
        scratch_shapes=[dma((4,))],
        compiler_params=pltpu.CompilerParams(has_side_effects=True, vmem_limit_bytes=4 << 20),
        name="store",
    )(*results)


def body(blocks, queries, keys, values, out_grad, block_list, positions):
    tokens, _, depth = queries.shape
    if blocks == 8:
        return tuple(quad(blocks, block_list, positions, queries, keys, values, out_grad))
    base = positions[0] - lax.axis_index("head") * tokens
    cosine, sine = tables(base + jnp.arange(BLOCK, dtype=jnp.int32), depth)
    return tuple(flow(blocks, block_list[0], queries, keys, values, out_grad, cosine, sine))


def solution(mesh):
    spec = P(("groups", "blk", "head"), None, None)
    in_specs = (spec, spec, spec, spec, P(("groups", "blk"), None), P(("groups", "blk", "head")))
    run = functools.partial(body, mesh.shape["blk"])
    return jax.shard_map(run, mesh=mesh, in_specs=in_specs, out_specs=(spec,) * 4, check_vma=False)
```

```python
import functools
import math

import jax
import jax.numpy as jnp
import numpy as np
from jax import lax
from jax.experimental import pallas as pl
from jax.experimental.pallas import tpu as pltpu
from jax.sharding import PartitionSpec as P

BLOCK = 128
ROPE_BASE = 10000.0
NEG_FILL = -1e30
LAG = 4
SKEW = 4
EARLY = ()


def tables(place, width):
    half = width // 2
    exponent = 2.0 * jnp.arange(half, dtype=jnp.float32) / width
    frequency = ROPE_BASE ** (-exponent)
    angle = place.astype(jnp.float32)[:, None] * frequency[None, :]
    cosine, sine = jnp.cos(angle), jnp.sin(angle)
    return jnp.concatenate([cosine, cosine], -1), jnp.concatenate([-sine, sine], -1)


def flow_kernel(
    blocks, inner, width, group, scale,
    list_ref, q_raw, k_raw, v_raw, g_raw, cos_ref, sin_ref, out_raw, qg_raw, kg_raw, vg_raw, *scratch,
):
    tokens, heads, depth = q_raw.shape
    heads = heads // 2
    key_heads = k_raw.shape[1] // 2
    outer = blocks // inner
    rows = group * BLOCK
    f32, low = jnp.float32, jnp.bfloat16
    nt = (((1,), (1,)), ((), ()))
    kv = scratch[:key_heads]
    (q_in, g_in, kv_in, out_home, qg_home, kvg_home, q_full, g_full, out_full, qg_full, kvg, k_all, v_all, part, own, y_send, y_part, z_send, z_part, acc, total_kv,
     core_send, core_recv, gz_send, gz_recv, gy_send, gy_recv, ry_send, ry_recv, rz_send, rz_recv) = scratch[key_heads:]

    me = lax.axis_index("blk")
    core = lax.axis_index("head")
    other = 1 - core
    z, y = me // inner, me % inner
    up, down = {"blk": me + inner}, {"blk": me - inner}
    side = {"blk": z * inner + (inner - 1 - y)}
    twin = {"head": other}
    mesh_id = pl.DeviceIdType.MESH
    mine = pl.ds(pl.multiple_of(core * tokens, tokens), tokens)
    theirs = pl.ds(pl.multiple_of(other * tokens, tokens), tokens)

    def remote(source, target, send, recv, device):
        return pltpu.make_async_remote_copy(
            src_ref=source, dst_ref=target, send_sem=send, recv_sem=recv, device_id=device, device_id_type=mesh_id
        )

    def repeat(count, step):
        if count <= 4:
            for index in range(count):
                step(index)
        else:
            lax.fori_loop(0, count, lambda index, carry: (step(index), carry)[1], 0)

    barrier = pltpu.get_barrier_semaphore()
    pl.semaphore_signal(barrier, inc=1, device_id=twin, device_id_type=mesh_id)
    if inner > 1:
        pl.semaphore_signal(barrier, inc=1, device_id=side, device_id_type=mesh_id)

    @pl.when(z > 0)
    def _():
        pl.semaphore_signal(barrier, inc=1, device_id=down, device_id_type=mesh_id)

    @pl.when(z < outer - 1)
    def _():
        pl.semaphore_signal(barrier, inc=1, device_id=up, device_id_type=mesh_id)

    peers = (2 if inner > 1 else 1) + (z + outer - 1) // outer + (2 * outer - 2 - z) // outer
    pl.semaphore_wait(barrier, peers)

    half = depth // 2
    step_tokens = 16

    def turn(x, place, sign):
        cosine, sine = cos_ref[place, :], sin_ref[place, :]
        swapped = pltpu.roll(x, half, x.ndim - 1)
        return x * cosine[None] + swapped * (sign * sine)[None]

    def bring(raw, write, rotate):
        for start in range(0, tokens, step_tokens):
            x = jnp.transpose(raw[start : start + step_tokens].astype(f32), (1, 0, 2))
            if rotate:
                place = pl.ds(pl.multiple_of(core * tokens + start, step_tokens), step_tokens)
                x = turn(x, place, 1.0)
            write(slice(start, start + step_tokens), x.astype(low))

    def take(read, raw):
        for start in range(0, tokens, step_tokens):
            x = read(slice(start, start + step_tokens)).astype(f32)
            raw[start : start + step_tokens] = jnp.transpose(x, (1, 0, 2)).astype(low)

    def write_to(ref, lane=None):
        def write(place, x):
            if lane is None:
                ref[:, place, :] = x
            else:
                ref[:, lane, place, :] = x

        return write

    bring(k_raw, write_to(kv_in, 0), True)
    bring(v_raw, write_to(kv_in, 1), False)
    swaps = []
    for h in range(key_heads):
        swaps.append(
            remote(kv_in.at[other * key_heads + h], kv[h].at[me, :, mine, :], core_send.at[h], core_recv.at[h], twin)
        )
    k = key_heads
    swaps.append(
        remote(q_in.at[pl.ds(other * heads, heads)], q_full.at[:, mine, :], core_send.at[k], core_recv.at[k], twin)
    )
    swaps.append(
        remote(g_in.at[pl.ds(other * heads, heads)], g_full.at[:, mine, :], core_send.at[k + 1], core_recv.at[k + 1], twin)
    )
    for copy in swaps[:key_heads]:
        copy.start()
    for h in range(key_heads):
        kv[h][me, :, mine, :] = kv_in[core * key_heads + h]

    def bring_queries():
        bring(q_raw, write_to(q_in), True)
        swaps[key_heads].start()
        bring(g_raw, write_to(g_in), False)
        swaps[key_heads + 1].start()
        q_full[:, mine, :] = q_in[pl.ds(core * heads, heads)]
        g_full[:, mine, :] = g_in[pl.ds(core * heads, heads)]
        part[width] = jnp.zeros(part.shape[1:], part.dtype)

    def early(h):
        return inner > 1 and h in EARLY

    def lanes(h):
        return 2 if early(h) else 1

    def column(lane):
        return y if lane == 0 else inner - 1 - y

    def gather_z(s, h, lane):
        view = kv[h].at[(z - s) * inner + column(lane)]
        return remote(view, view, gz_send.at[s, h, lane], gz_recv.at[s, h, lane], up)

    def arrived_z(s, h, lane):
        view = kv[h].at[(z - s) * inner + column(lane)]
        return remote(view, view, gz_send.at[s - 1, h, lane], gz_recv.at[s - 1, h, lane], down)

    def gather_y(s, h):
        view = kv[h].at[(z - s) * inner + column(0)]
        return remote(view, view, gy_send.at[s, h], gy_recv.at[s, h], side)

    def arrived_y(s, h):
        view = kv[h].at[(z - s) * inner + column(1)]
        return remote(view, view, gy_send.at[s, h], gy_recv.at[s, h], side)

    def crosses(s, h):
        return inner > 1 and (s == 0 or not early(h))

    def sends_y(s, h):
        return (z >= s) & (y == 0) if s == 0 and not early(h) else z >= s

    def takes_y(s, h):
        return (z >= s) & (y == 1) if s == 0 and not early(h) else z >= s

    def forward(s, h):
        if s == 0:
            swaps[h].wait_recv()
            if early(h):
                gather_y(0, h).start()
        for lane in range(lanes(h)):
            if s > 0:

                @pl.when(z >= s)
                def _():
                    arrived_z(s, h, lane).wait_recv()

            elif lane == 1:
                arrived_y(0, h).wait_recv()

            @pl.when((z >= s) & (z < outer - 1))
            def _():
                gather_z(s, h, lane).start()

        if crosses(s, h) and not early(h):

            @pl.when(sends_y(s, h))
            def _():
                gather_y(s, h).start()

    def attend(h):
        if inner > 1 and not early(h):
            for s in range(outer):

                @pl.when(takes_y(s, h))
                def _():
                    arrived_y(s, h).wait_recv()

        if h == 0:
            swaps[key_heads].wait_recv()
            swaps[key_heads + 1].wait_recv()
        first = h * group
        for entry in range(width):
            block = jnp.maximum(list_ref[entry], 0)
            k_all[pl.ds(entry * BLOCK, BLOCK), :] = kv[h][block, 0]
            v_all[pl.ds(entry * BLOCK, BLOCK), :] = kv[h][block, 1]
        q = q_full[pl.ds(first, group)].reshape(rows, depth)
        g = g_full[pl.ds(first, group)].reshape(rows, depth)
        kk, vv = k_all[...], v_all[...]
        score = lax.dot_general(kk, q, nt, preferred_element_type=f32) * scale
        prob_grad = lax.dot_general(vv, g, nt, preferred_element_type=f32)
        key_row = lax.broadcasted_iota(jnp.int32, (BLOCK, rows), 0)
        query_row = lax.broadcasted_iota(jnp.int32, (BLOCK, rows), 1) % BLOCK
        causal = key_row <= query_row
        pieces = []
        for entry in range(width):
            block = list_ref[entry]
            allowed = jnp.logical_and(block >= 0, jnp.logical_or(block != me, causal))
            pieces.append(jnp.where(allowed, score[entry * BLOCK : (entry + 1) * BLOCK], NEG_FILL))
        score = jnp.concatenate(pieces, axis=0)
        best = jnp.max(score, axis=0, keepdims=True)
        weights = jnp.exp(score - best)
        inverse = 1.0 / jnp.sum(weights, axis=0, keepdims=True)
        out_t = jnp.dot(vv.T, weights.astype(low), preferred_element_type=f32) * inverse
        out_low = out_t.astype(low)
        out_full[pl.ds(first, group)] = out_t.T.astype(low).reshape(group, BLOCK, depth)
        delta = jnp.sum(g.astype(f32).T * out_low.astype(f32), axis=0, keepdims=True)
        prob = weights * inverse
        score_grad = (prob * (prob_grad - delta)).astype(low)
        value_part = jnp.dot(prob.astype(low), g, preferred_element_type=f32).astype(low)
        key_part = (jnp.dot(score_grad, q, preferred_element_type=f32) * scale).astype(low)
        for entry in range(width):
            part[entry, 0] = key_part[entry * BLOCK : (entry + 1) * BLOCK]
            part[entry, 1] = value_part[entry * BLOCK : (entry + 1) * BLOCK]

        def place(block):
            slot = jnp.int32(width)
            for entry in range(width):
                slot = jnp.where(list_ref[entry] == block, entry, slot)
            return slot

        def spread(zd):
            if inner > 1 and not early(h):

                @pl.when((zd < z) | ((zd == z) & (y == 1)))
                def _():
                    y_send[h, zd] = part[place(zd * inner + column(1))]
                    reduce_y(zd, h).start()

            for lane in range(lanes(h)):
                own[h, zd, lane] = part[place(zd * inner + column(lane))]

        repeat(outer, spread)
        qg = (jnp.dot(kk.T, score_grad, preferred_element_type=f32) * scale).T
        qg = qg.reshape(group, BLOCK, depth)
        half = depth // 2
        swapped = jnp.concatenate([qg[..., half:], qg[..., :half]], axis=-1)
        qg_full[pl.ds(first, group)] = (qg * cos_ref[...][None] - swapped * sin_ref[...][None]).astype(low)
        for copy in homeward(h):
            copy.start()
        out_home[pl.ds(core * heads + first, group)] = out_full[pl.ds(first, group), mine, :]
        qg_home[pl.ds(core * heads + first, group)] = qg_full[pl.ds(first, group), mine, :]

    def homeward(h):
        source, target = pl.ds(h * group, group), pl.ds(core * heads + h * group, group)
        a, b = key_heads + 2 + h, 2 * key_heads + 2 + h
        return (
            remote(out_full.at[source, theirs, :], out_home.at[target], core_send.at[a], core_recv.at[a], twin),
            remote(qg_full.at[source, theirs, :], qg_home.at[target], core_send.at[b], core_recv.at[b], twin),
        )

    def reduce_y(zd, h):
        return remote(y_send.at[h, zd], y_part.at[h, zd], ry_send.at[zd, h], ry_recv.at[zd, h], side)

    def reduce_z(zd, h, lane):
        return remote(
            z_send.at[h, zd, lane], z_part.at[h, zd, lane], rz_send.at[zd, h, lane], rz_recv.at[zd, h, lane], down
        )

    def reduce(h):
        def one(zd):
            for lane in reversed(range(lanes(h))):

                @pl.when(zd <= z)
                def _():
                    acc[...] = own[h, zd, lane].astype(f32)

                    if inner > 1 and not early(h):

                        @pl.when((zd < z) | (y == 0))
                        def _():
                            reduce_y(zd, h).wait_recv()
                            acc[...] += y_part[h, zd].astype(f32)

                    @pl.when(z < outer - 1)
                    def _():
                        reduce_z(zd, h, lane).wait_recv()
                        acc[...] += z_part[h, zd, lane].astype(f32)

                    @pl.when(zd < z)
                    def _():
                        z_send[h, zd, lane] = acc[...].astype(low)
                        reduce_z(zd, h, lane).start()

                    @pl.when(zd == z)
                    def _():
                        if lane == 1:
                            y_send[h, zd] = acc[...].astype(low)
                            reduce_y(zd, h).start()
                        else:
                            total_kv[h] = acc[...]

        repeat(outer, one)

    def settle(h):
        if early(h):
            reduce_y(z, h).wait_recv()
            total_kv[h] += y_part[h, z].astype(f32)

    moves = sorted((h + SKEW * s, s, h) for h in range(key_heads) for s in range(outer))
    ends = [moves.index((h + SKEW * (outer - 1), outer - 1, h)) for h in range(key_heads)]
    ready = [min(end + LAG, len(moves) - 1) for end in ends]
    for step, (_, s, h) in enumerate(moves):
        forward(s, h)
        if step == key_heads - 1:
            bring_queries()
        for done in range(key_heads):
            if ready[done] == step:
                attend(done)
                if done >= 1:
                    reduce(done - 1)
    for h in range(key_heads):
        for copy in homeward(h):
            copy.wait()
    take(lambda place: out_home[:, place, :], out_raw)
    take(lambda place: qg_home[:, place, :], qg_raw)
    reduce(key_heads - 1)
    for h in range(key_heads):
        settle(h)

    key_total = total_kv[:, 0]
    half = depth // 2
    swapped = jnp.concatenate([key_total[..., half:], key_total[..., :half]], axis=-1)
    kvg[:, 0] = (key_total * cos_ref[...][None] - swapped * sin_ref[...][None]).astype(low)
    kvg[:, 1] = total_kv[:, 1].astype(low)
    final = 3 * key_heads + 2
    target = pl.ds(core * key_heads, key_heads)
    closing = remote(kvg.at[:, :, theirs, :], kvg_home.at[target], core_send.at[final], core_recv.at[final], twin)
    closing.start()
    kvg_home[target] = kvg[:, :, mine, :]

    for copy in swaps:
        copy.wait_send()
    for h in range(key_heads):
        for s in range(outer):

            for lane in range(lanes(h)):

                @pl.when((z >= s) & (z < outer - 1))
                def _():
                    gather_z(s, h, lane).wait_send()

                @pl.when(s < z)
                def _():
                    reduce_z(s, h, lane).wait_send()

            if crosses(s, h):

                @pl.when(sends_y(s, h))
                def _():
                    gather_y(s, h).wait_send()

            if inner > 1 and not early(h):

                @pl.when((s < z) | ((s == z) & (y == 1)))
                def _():
                    reduce_y(s, h).wait_send()

        if early(h):
            reduce_y(z, h).wait_send()
    closing.wait()
    take(lambda place: kvg_home[:, 0, place, :], kg_raw)
    take(lambda place: kvg_home[:, 1, place, :], vg_raw)


def flow(blocks, list_row, q, k, v, g, cosine, sine):
    tokens, heads, depth = q.shape
    key_heads = k.shape[1] // 2
    group = heads // k.shape[1]
    width = list_row.shape[0]
    inner = 2 if blocks == 8 else 1
    outer = blocks // inner
    low, f32 = jnp.bfloat16, jnp.float32
    vmem, dma = pltpu.VMEM, pltpu.SemaphoreType.DMA
    whole = pl.BlockSpec(memory_space=pltpu.VMEM)
    half_heads = (heads // 2, BLOCK, depth)
    tile = (2, BLOCK, depth)
    sided = (key_heads, outer if inner > 1 else 1) + tile
    flags = (outer, key_heads)
    scratch = [vmem((blocks,) + tile, low)] * key_heads
    home = [vmem((heads, tokens, depth), low)] * 2 + [vmem((2 * key_heads, 2, tokens, depth), low)]
    scratch += home + home + [vmem(half_heads, low)] * 4
    scratch += [vmem((key_heads,) + tile, low)]
    scratch += [vmem((width * BLOCK, depth), low)] * 2
    scratch += [vmem((width + 1,) + tile, low)]
    scratch += [vmem((key_heads, outer, inner) + tile, low)]
    scratch += [vmem(sided, low)] * 2
    scratch += [vmem((key_heads, outer, inner) + tile, low)] * 2
    scratch += [vmem(tile, f32), vmem((key_heads,) + tile, f32)]
    scratch += [dma((3 * key_heads + 3,))] * 2
    scratch += [dma(flags + (inner,))] * 2 + [dma(flags)] * 4 + [dma(flags + (inner,))] * 2
    return pl.pallas_call(
        functools.partial(flow_kernel, blocks, inner, width, group, 1.0 / math.sqrt(depth)),
        in_specs=[pl.BlockSpec(memory_space=pltpu.SMEM)] + [whole] * 6,
        out_specs=[whole] * 4,
        out_shape=[jax.ShapeDtypeStruct(x.shape, low) for x in (q, q, k, k)],
        scratch_shapes=scratch,
        compiler_params=pltpu.CompilerParams(
            collective_id=0, has_side_effects=True, vmem_limit_bytes=60 << 20
        ),
        name="flow",
    )(list_row, q, k, v, g, cosine, sine)


def quad_kernel(
    outer, width, group, scale,
    list_ref, place_ref, k_far, v_far, token_far, base_far, q_far, g_far, out_raw, qg_raw, kg_raw, vg_raw, *scratch,
):
    tokens, key_heads, depth = k_far.shape
    local = key_heads // 4
    heads = local * group
    rows = group * BLOCK
    f32, low = jnp.float32, jnp.bfloat16
    nt = (((1,), (1,)), ((), ()))
    kv = scratch[:local]
    (q_raw, g_raw, kv_in, q_in, g_in, q_full, g_full, out_full, qg_full, out_home, qg_home, kvg, kvg_home, k_all, v_all, part,
     own, z_send, z_part, acc, cos_ref, sin_ref, note,
     far_sem, note_send, note_recv, kv_send, kv_recv, q_send, q_recv, g_send, g_recv, out_send, out_recv, qg_send, qg_recv,
     home_send, home_recv, gz_send, gz_recv, rz_send, rz_recv, relay_recv, relay, pending, k_raw, v_raw, token_ref, base_ref, out_turned, slopes) = scratch[local:]

    me = lax.axis_index("blk")
    core = lax.axis_index("head")
    z, y = me // 2, me % 2
    quarter = 2 * y + core
    mesh_id = pl.DeviceIdType.MESH
    mine = pl.ds(pl.multiple_of(core * tokens, tokens), tokens)
    theirs = pl.ds(pl.multiple_of((1 - core) * tokens, tokens), tokens)
    half = depth // 2
    step_tokens = 16

    def row_of(side):
        return y if side == 0 else 1 - y

    def core_of(cross):
        return core if cross == 0 else 1 - core

    def peer(side, cross):
        return {"blk": 2 * z + row_of(side), "head": core_of(cross)}

    def quarter_of(side, cross):
        return 2 * row_of(side) + core_of(cross)

    def level(other):
        return {"blk": 2 * other + y}

    def remote(source, target, send, recv, device):
        return pltpu.make_async_remote_copy(
            src_ref=source, dst_ref=target, send_sem=send, recv_sem=recv, device_id=device, device_id_type=mesh_id
        )

    peers = ((0, 1), (1, 0), (1, 1))
    barrier = pltpu.get_barrier_semaphore()
    for side, cross in peers:
        pl.semaphore_signal(barrier, inc=1, device_id=peer(side, cross), device_id_type=mesh_id)
    for other in range(outer):

        @pl.when(z != other)
        def _():
            pl.semaphore_signal(barrier, inc=1, device_id=level(other), device_id_type=mesh_id)

    def bring_in(index, far, near):
        copy = pltpu.make_async_copy(far, near, far_sem.at[index])
        copy.start()
        return copy

    far_token, far_base = bring_in(0, token_far, token_ref), bring_in(1, base_far, base_ref)
    far_k, far_v = bring_in(2, k_far, k_raw), bring_in(3, v_far, v_raw)
    far_q, far_g = bring_in(4, q_far, q_raw), bring_in(5, g_far, g_raw)

    def angles(side, depth_of):
        first = base_ref[depth_of]
        cosine, sine = first[0:1], first[1:2]
        cos_ref[side] = token_ref[0] * cosine - token_ref[1] * sine
        sin_ref[side] = token_ref[1] * cosine + token_ref[0] * sine

    depth_here = place_ref[0] // BLOCK
    far_token.wait()
    far_base.wait()
    angles(0, depth_here)
    for entry in range(width):
        note[0, entry] = list_ref[0, entry]
    note[0, width] = depth_here

    def turn(x, place, sign):
        cosine, sine = cos_ref[0, place, :], sin_ref[0, place, :]
        swapped = pltpu.roll(x, half, x.ndim - 1)
        return x * cosine[None] + swapped * (sign * sine)[None]

    def bring(raw, write, rotate):
        for start in range(0, tokens, step_tokens):
            x = jnp.transpose(raw[start : start + step_tokens].astype(f32), (1, 0, 2))
            if rotate:
                place = pl.ds(pl.multiple_of(core * tokens + start, step_tokens), step_tokens)
                x = turn(x, place, 1.0)
            write(slice(start, start + step_tokens), x.astype(low))

    def take(read, raw):
        for start in range(0, tokens, step_tokens):
            x = read(slice(start, start + step_tokens)).astype(f32)
            raw[start : start + step_tokens] = jnp.transpose(x, (1, 0, 2)).astype(low)

    def write_to(ref, lane=None):
        def write(place, x):
            if lane is None:
                ref[:, place, :] = x
            else:
                ref[:, lane, place, :] = x

        return write

    def send_note():
        return remote(note.at[0], note.at[1], note_send, note_recv, peer(1, 0))

    def swap_kv(h, r):
        return remote(
            kv_in.at[quarter_of(*peers[r]) * local + h], kv[h].at[me, :, mine, :], kv_send.at[h, r], kv_recv.at[h, r], peer(*peers[r])
        )

    def swap_q(h, r):
        source = pl.ds(quarter_of(*peers[r]) * heads + h * group, group)
        target = q_full.at[peers[r][0], pl.ds(h * group, group), mine, :]
        return remote(q_in.at[source], target, q_send.at[h, r], q_recv.at[h, r], peer(*peers[r]))

    def swap_g(h, r):
        source = pl.ds(quarter_of(*peers[r]) * heads + h * group, group)
        target = g_full.at[peers[r][0], pl.ds(h * group, group), mine, :]
        return remote(g_in.at[source], target, g_send.at[h, r], g_recv.at[h, r], peer(*peers[r]))

    def gather_z(h, side, far):
        view = kv[h].at[2 * z + row_of(side)]
        return remote(view, view, gz_send.at[h, side, far], gz_recv.at[h, side, z], level(far))

    def arrived_z(h, side, near):
        view = kv[h].at[2 * near + row_of(side)]
        return remote(view, view, gz_send.at[h, side, near], gz_recv.at[h, side, near], level(near))

    def reduce_z(h, side, near):
        return remote(
            z_send.at[h, near, side], z_part.at[h, z, side], rz_send.at[h, side, near], rz_recv.at[h, side, z], level(near)
        )

    def returned_z(h, side, far):
        return remote(
            z_send.at[h, far, side], z_part.at[h, far, side], rz_send.at[h, side, far], rz_recv.at[h, side, far], level(far)
        )

    last, relay_level = outer - 1, outer - 2

    def upward(h, side):
        for far in reversed(range(1, outer)):

            @pl.when((z < far) & (far - z < last))
            def _():
                gather_z(h, side, far).start()

    def relayed_up(h, side):
        view = kv[h].at[row_of(side)]
        return remote(view, view, gz_send.at[h, side, 0], gz_recv.at[h, side, 0], level(last))

    def pass_up(h, side):
        @pl.when(z == relay_level)
        def _():
            arrived_z(h, side, 0).wait_recv()
            relayed_up(h, side).start()

    def relayed_down(h, side):
        return remote(
            z_send.at[h, 0, side], relay.at[h, side], rz_send.at[h, side, 0], relay_recv.at[h, side], level(relay_level)
        )

    def pass_down(h):
        for lane in (1, 0):

            @pl.when(z == relay_level)
            def _():
                relayed_down(h, lane).wait_recv()
                z_send[h, 0, lane] = (pending[h, lane] + relay[h, lane].astype(f32)).astype(low)
                reduce_z(h, lane, 0).start()

    far_k.wait()
    bring(k_raw, write_to(kv_in, 0), True)
    far_v.wait()
    bring(v_raw, write_to(kv_in, 1), False)
    pl.semaphore_wait(barrier, outer + 2)
    for h in range(local):
        for r in range(3):
            swap_kv(h, r).start()
    send_note().start()
    for h in range(local):
        kv[h][me, :, mine, :] = kv_in[quarter * local + h]
    swap_kv(0, 0).wait_recv()
    upward(0, 0)
    far_q.wait()
    bring(q_raw, write_to(q_in), True)
    for r in range(3):
        swap_q(0, r).start()
    for r in (1, 2):
        swap_kv(0, r).wait_recv()
    upward(0, 1)
    swap_kv(1, 0).wait_recv()
    upward(1, 0)
    for r in (1, 2):
        swap_kv(1, r).wait_recv()
    upward(1, 1)
    far_g.wait()
    bring(g_raw, write_to(g_in), False)
    for r in range(3):
        swap_g(0, r).start()
    for h in range(1, local):
        for r in range(3):
            swap_q(h, r).start()
            swap_g(h, r).start()
    q_full[0, :, mine, :] = q_in[pl.ds(quarter * heads, heads)]
    g_full[0, :, mine, :] = g_in[pl.ds(quarter * heads, heads)]
    for side in range(2):
        part[side, width] = jnp.zeros(part.shape[2:], part.dtype)
    send_note().wait_recv()
    angles(1, note[1, width])

    def homeward(h, side):
        copies = []
        for r in range(3):
            if peers[r][0] != side:
                continue
            place = mine if peers[r][1] == 0 else theirs
            source = pl.ds(h * group, group)
            target = pl.ds(quarter * heads + h * group, group)
            copies.append(
                remote(out_full.at[side, source, place, :], out_home.at[target], out_send.at[h, r], out_recv.at[h, r], peer(*peers[r]))
            )
            copies.append(
                remote(qg_full.at[side, source, place, :], qg_home.at[target], qg_send.at[h, r], qg_recv.at[h, r], peer(*peers[r]))
            )
        return copies

    def attend(h, side):
        if side == 1:
            for near in range(outer - 1):
                for lane in range(2):

                    @pl.when((near < z) & ((near > 0) | (z != relay_level)))
                    def _():
                        arrived_z(h, lane, near).wait_recv()

            for r in range(3):
                swap_q(h, r).wait_recv()
                swap_g(h, r).wait_recv()
        block_here = 2 * z + row_of(side)
        first = h * group
        for entry in range(width):
            block = jnp.maximum(note[side, entry], 0)
            k_all[side, pl.ds(entry * BLOCK, BLOCK), :] = kv[h][block, 0]
            v_all[pl.ds(entry * BLOCK, BLOCK), :] = kv[h][block, 1]
        q = q_full[side, pl.ds(first, group)].reshape(rows, depth)
        g = g_full[side, pl.ds(first, group)].reshape(rows, depth)
        kk, vv = k_all[side], v_all[...]
        score = lax.dot_general(kk, q, nt, preferred_element_type=f32) * scale
        prob_grad = lax.dot_general(vv, g, nt, preferred_element_type=f32)
        key_row = lax.broadcasted_iota(jnp.int32, (BLOCK, rows), 0)
        query_row = lax.broadcasted_iota(jnp.int32, (BLOCK, rows), 1) % BLOCK
        causal = key_row <= query_row
        pieces = []
        for entry in range(width):
            block = note[side, entry]
            allowed = jnp.logical_and(block >= 0, jnp.logical_or(block != block_here, causal))
            pieces.append(jnp.where(allowed, score[entry * BLOCK : (entry + 1) * BLOCK], NEG_FILL))
        score = jnp.concatenate(pieces, axis=0)
        best = jnp.max(score, axis=0, keepdims=True)
        weights = jnp.exp(score - best)
        inverse = 1.0 / jnp.sum(weights, axis=0, keepdims=True)
        out_t = jnp.dot(vv.T, weights.astype(low), preferred_element_type=f32) * inverse
        out_low = out_t.astype(low)
        out_turned[side] = out_low
        delta = jnp.sum(g.astype(f32).T * out_low.astype(f32), axis=0, keepdims=True)
        prob = weights * inverse
        score_grad = (prob * (prob_grad - delta)).astype(low)
        slopes[side] = score_grad
        value_part = jnp.dot(prob.astype(low), g, preferred_element_type=f32).astype(low)
        key_part = (jnp.dot(score_grad, q, preferred_element_type=f32) * scale).astype(low)
        for entry in range(width):
            part[side, entry, 0] = key_part[entry * BLOCK : (entry + 1) * BLOCK]
            part[side, entry, 1] = value_part[entry * BLOCK : (entry + 1) * BLOCK]

    def finish(h, side):
        first = h * group
        out_full[side, pl.ds(first, group)] = out_turned[side].astype(f32).T.astype(low).reshape(group, BLOCK, depth)
        qg = (jnp.dot(k_all[side].T, slopes[side], preferred_element_type=f32) * scale).T
        qg = qg.reshape(group, BLOCK, depth)
        swapped = jnp.concatenate([qg[..., half:], qg[..., :half]], axis=-1)
        qg_full[side, pl.ds(first, group)] = (qg * cos_ref[side][None] - swapped * sin_ref[side][None]).astype(low)
        for copy in homeward(h, side):
            copy.start()
        if side == 0:
            target = pl.ds(quarter * heads + first, group)
            out_home[target] = out_full[0, pl.ds(first, group), mine, :]
            qg_home[target] = qg_full[0, pl.ds(first, group), mine, :]

    def slot_of(side, block):
        slot = jnp.int32(width)
        for entry in range(width):
            slot = jnp.where(note[side, entry] == block, entry, slot)
        return slot

    def spread(h):
        for near in range(outer):
            for lane in (1, 0):

                @pl.when(near <= z)
                def _():
                    block = 2 * near + row_of(lane)
                    total = part[0, slot_of(0, block)].astype(f32) + part[1, slot_of(1, block)].astype(f32)

                    @pl.when((near < z) & ((near > 0) | (z < relay_level)))
                    def _():
                        z_send[h, near, lane] = total.astype(low)
                        reduce_z(h, lane, near).start()

                    if near == 0:

                        @pl.when(z == relay_level)
                        def _():
                            pending[h, lane] = total

                        @pl.when(z == last)
                        def _():
                            z_send[h, near, lane] = total.astype(low)
                            relayed_down(h, lane).start()

                    @pl.when(near == z)
                    def _():
                        own[h, lane] = total

    def kv_home(h, r):
        side, cross = peers[r]
        place = mine if cross == 0 else theirs
        return remote(
            kvg.at[h, side, :, place, :], kvg_home.at[quarter * local + h], home_send.at[h, r], home_recv.at[h, r], peer(side, cross)
        )

    def settle(h):
        for lane in (1, 0):
            acc[...] = own[h, lane]
            for far in range(1, outer):

                @pl.when((z < far) & (far - z < last))
                def _():
                    returned_z(h, lane, far).wait_recv()
                    acc[...] += z_part[h, far, lane].astype(f32)

            key_total = acc[0]
            swapped = jnp.concatenate([key_total[..., half:], key_total[..., :half]], axis=-1)
            kvg[h, lane, 0] = (key_total * cos_ref[lane] - swapped * sin_ref[lane]).astype(low)
            kvg[h, lane, 1] = acc[1].astype(low)
            for r in range(3):
                if peers[r][0] == lane:
                    kv_home(h, r).start()
        kvg_home[quarter * local + h] = kvg[h, 0, :, mine, :]

    pass_up(0, 0)
    pass_up(0, 1)
    for h in range(local):
        attend(h, 1)
        if h + 1 < local:
            pass_up(h + 1, 0)
        if h > 0:
            pass_down(h - 1)
        attend(h, 0)
        if h + 1 < local:
            pass_up(h + 1, 1)
        spread(h)
        finish(h, 1)
        finish(h, 0)
    pass_down(local - 1)
    for h in range(local - 1):
        settle(h)
    for h in range(local):
        for side in range(2):
            for copy in homeward(h, side):
                copy.wait()
    take(lambda place: out_home[:, place, :], out_raw)
    take(lambda place: qg_home[:, place, :], qg_raw)
    settle(local - 1)

    send_note().wait_send()
    for h in range(local):
        for r in range(3):
            swap_kv(h, r).wait_send()
            swap_q(h, r).wait_send()
            swap_g(h, r).wait_send()
        for side in range(2):
            for far in range(1, outer):

                @pl.when((z < far) & (far - z < last))
                def _():
                    gather_z(h, side, far).wait_send()

            @pl.when(z == relay_level)
            def _():
                relayed_up(h, side).wait_send()

            for near in range(outer - 1):

                @pl.when((near < z) & (z - near < last))
                def _():
                    reduce_z(h, side, near).wait_send()

            @pl.when(z == last)
            def _():
                relayed_down(h, side).wait_send()

    for h in range(local):
        for r in range(3):
            kv_home(h, r).wait()
    take(lambda place: kvg_home[:, 0, place, :], kg_raw)
    take(lambda place: kvg_home[:, 1, place, :], vg_raw)


def store_kernel(*refs):
    done = refs[8]
    copies = [pltpu.make_async_copy(refs[index], refs[4 + index], done.at[index]) for index in range(4)]
    for copy in copies:
        copy.start()
    for copy in copies:
        copy.wait()


def angle_tables(width, depth):
    half = depth // 2
    frequency = ROPE_BASE ** (-2.0 * np.arange(half) / depth)

    def pair(place):
        angle = place[:, None] * frequency[None, :]
        cosine, sine = np.cos(angle), np.sin(angle)
        return np.stack([np.concatenate([cosine, cosine], -1), np.concatenate([-sine, sine], -1)]).astype(np.float32)

    token = pair(np.arange(BLOCK, dtype=np.float64))
    base = pair(np.arange(width, dtype=np.float64) * BLOCK)
    return token, np.moveaxis(base, 0, 1)


def quad(blocks, list_rows, places, q, k, v, g):
    tokens, heads, depth = q.shape
    key_heads = k.shape[1]
    group = heads // key_heads
    local = key_heads // 4
    width = list_rows.shape[1]
    outer = blocks // 2
    low, f32 = jnp.bfloat16, jnp.float32
    vmem, dma = pltpu.VMEM, pltpu.SemaphoreType.DMA
    whole = pl.BlockSpec(memory_space=pltpu.VMEM)
    scalar = pl.BlockSpec(memory_space=pltpu.SMEM)
    distant = pl.BlockSpec(memory_space=pl.ANY)
    token, base = angle_tables(width, depth)
    tile = (2, BLOCK, depth)
    full = (2, local * group, BLOCK, depth)
    scratch = [vmem((blocks,) + tile, low)] * local
    scratch += [vmem(q.shape, low)] * 2
    scratch += [vmem((key_heads, 2, tokens, depth), low)] + [vmem((heads, tokens, depth), low)] * 2
    scratch += [vmem(full, low)] * 4 + [vmem((heads, tokens, depth), low)] * 2
    scratch += [vmem((local, 2) + tile, low), vmem((key_heads, 2, tokens, depth), low)]
    scratch += [vmem((2, width * BLOCK, depth), low), vmem((width * BLOCK, depth), low)]
    scratch += [vmem((2, width + 1) + tile, low), vmem((local, 2) + tile, f32)]
    scratch += [vmem((local, outer, 2) + tile, low)] * 2
    scratch += [vmem(tile, f32)] + [vmem((2, BLOCK, depth), f32)] * 2
    scratch += [pltpu.SMEM((2, 2 * width), jnp.int32)]
    scratch += [dma((6,)), dma, dma] + [dma((local, 3))] * 12 + [dma((local, 2, outer))] * 4
    scratch += [dma((local, 2)), vmem((local, 2) + tile, low), vmem((local, 2) + tile, f32)]
    scratch += [vmem(k.shape, low)] * 2 + [vmem(token.shape, f32), vmem(base.shape, f32)]
    scratch += [vmem((2, depth, group * BLOCK), low), vmem((2, width * BLOCK, group * BLOCK), low)]
    results = pl.pallas_call(
        functools.partial(quad_kernel, outer, width, group, 1.0 / math.sqrt(depth)),
        in_specs=[scalar] * 2 + [distant] * 6,
        out_specs=[whole] * 4,
        out_shape=[vmem(x.shape, low) for x in (q, q, k, k)],
        scratch_shapes=scratch,
        compiler_params=pltpu.CompilerParams(
            collective_id=1, has_side_effects=True, vmem_limit_bytes=60 << 20
        ),
        name="quad_flow",
    )(list_rows, places, k, v, jnp.asarray(token), jnp.asarray(base), q, g)
    return pl.pallas_call(
        store_kernel,
        in_specs=[distant] * 4,
        out_specs=[distant] * 4,
        out_shape=[jax.ShapeDtypeStruct(x.shape, low) for x in (q, q, k, k)],
        scratch_shapes=[dma((4,))],
        compiler_params=pltpu.CompilerParams(has_side_effects=True, vmem_limit_bytes=4 << 20),
        name="store",
    )(*results)


def body(blocks, queries, keys, values, out_grad, block_list, positions):
    tokens, _, depth = queries.shape
    if blocks == 8:
        return tuple(quad(blocks, block_list, positions, queries, keys, values, out_grad))
    base = positions[0] - lax.axis_index("head") * tokens
    cosine, sine = tables(base + jnp.arange(BLOCK, dtype=jnp.int32), depth)
    return tuple(flow(blocks, block_list[0], queries, keys, values, out_grad, cosine, sine))


def solution(mesh):
    spec = P(("groups", "blk", "head"), None, None)
    in_specs = (spec, spec, spec, spec, P(("groups", "blk"), None), P(("groups", "blk", "head")))
    run = functools.partial(body, mesh.shape["blk"])
    return jax.shard_map(run, mesh=mesh, in_specs=in_specs, out_specs=(spec,) * 4, check_vma=False)
```

```python
import functools
import math

import jax
import jax.numpy as jnp
import numpy as np
from jax import lax
from jax.experimental import pallas as pl
from jax.experimental.pallas import tpu as pltpu
from jax.sharding import PartitionSpec as P

BLOCK = 128
ROPE_BASE = 10000.0
NEG_FILL = -1e30
LAG = 4
SKEW = 4
EARLY = ()


def tables(place, width):
    half = width // 2
    exponent = 2.0 * jnp.arange(half, dtype=jnp.float32) / width
    frequency = ROPE_BASE ** (-exponent)
    angle = place.astype(jnp.float32)[:, None] * frequency[None, :]
    cosine, sine = jnp.cos(angle), jnp.sin(angle)
    return jnp.concatenate([cosine, cosine], -1), jnp.concatenate([-sine, sine], -1)


def flow_kernel(
    blocks, inner, width, group, scale,
    list_ref, q_raw, k_raw, v_raw, g_raw, cos_ref, sin_ref, out_raw, qg_raw, kg_raw, vg_raw, *scratch,
):
    tokens, heads, depth = q_raw.shape
    heads = heads // 2
    key_heads = k_raw.shape[1] // 2
    outer = blocks // inner
    rows = group * BLOCK
    f32, low = jnp.float32, jnp.bfloat16
    nt = (((1,), (1,)), ((), ()))
    kv = scratch[:key_heads]
    (q_in, g_in, kv_in, out_home, qg_home, kvg_home, q_full, g_full, out_full, qg_full, kvg, k_all, v_all, part, own, y_send, y_part, z_send, z_part, acc, total_kv,
     core_send, core_recv, gz_send, gz_recv, gy_send, gy_recv, ry_send, ry_recv, rz_send, rz_recv) = scratch[key_heads:]

    me = lax.axis_index("blk")
    core = lax.axis_index("head")
    other = 1 - core
    z, y = me // inner, me % inner
    up, down = {"blk": me + inner}, {"blk": me - inner}
    side = {"blk": z * inner + (inner - 1 - y)}
    twin = {"head": other}
    mesh_id = pl.DeviceIdType.MESH
    mine = pl.ds(pl.multiple_of(core * tokens, tokens), tokens)
    theirs = pl.ds(pl.multiple_of(other * tokens, tokens), tokens)

    def remote(source, target, send, recv, device):
        return pltpu.make_async_remote_copy(
            src_ref=source, dst_ref=target, send_sem=send, recv_sem=recv, device_id=device, device_id_type=mesh_id
        )

    def repeat(count, step):
        if count <= 4:
            for index in range(count):
                step(index)
        else:
            lax.fori_loop(0, count, lambda index, carry: (step(index), carry)[1], 0)

    barrier = pltpu.get_barrier_semaphore()
    pl.semaphore_signal(barrier, inc=1, device_id=twin, device_id_type=mesh_id)
    if inner > 1:
        pl.semaphore_signal(barrier, inc=1, device_id=side, device_id_type=mesh_id)

    @pl.when(z > 0)
    def _():
        pl.semaphore_signal(barrier, inc=1, device_id=down, device_id_type=mesh_id)

    @pl.when(z < outer - 1)
    def _():
        pl.semaphore_signal(barrier, inc=1, device_id=up, device_id_type=mesh_id)

    peers = (2 if inner > 1 else 1) + (z + outer - 1) // outer + (2 * outer - 2 - z) // outer
    pl.semaphore_wait(barrier, peers)

    half = depth // 2
    step_tokens = 16

    def turn(x, place, sign):
        cosine, sine = cos_ref[place, :], sin_ref[place, :]
        swapped = pltpu.roll(x, half, x.ndim - 1)
        return x * cosine[None] + swapped * (sign * sine)[None]

    def bring(raw, write, rotate):
        for start in range(0, tokens, step_tokens):
            x = jnp.transpose(raw[start : start + step_tokens].astype(f32), (1, 0, 2))
            if rotate:
                place = pl.ds(pl.multiple_of(core * tokens + start, step_tokens), step_tokens)
                x = turn(x, place, 1.0)
            write(slice(start, start + step_tokens), x.astype(low))

    def take(read, raw):
        for start in range(0, tokens, step_tokens):
            x = read(slice(start, start + step_tokens)).astype(f32)
            raw[start : start + step_tokens] = jnp.transpose(x, (1, 0, 2)).astype(low)

    def write_to(ref, lane=None):
        def write(place, x):
            if lane is None:
                ref[:, place, :] = x
            else:
                ref[:, lane, place, :] = x

        return write

    bring(k_raw, write_to(kv_in, 0), True)
    bring(v_raw, write_to(kv_in, 1), False)
    swaps = []
    for h in range(key_heads):
        swaps.append(
            remote(kv_in.at[other * key_heads + h], kv[h].at[me, :, mine, :], core_send.at[h], core_recv.at[h], twin)
        )
    k = key_heads
    swaps.append(
        remote(q_in.at[pl.ds(other * heads, heads)], q_full.at[:, mine, :], core_send.at[k], core_recv.at[k], twin)
    )
    swaps.append(
        remote(g_in.at[pl.ds(other * heads, heads)], g_full.at[:, mine, :], core_send.at[k + 1], core_recv.at[k + 1], twin)
    )
    for copy in swaps[:key_heads]:
        copy.start()
    for h in range(key_heads):
        kv[h][me, :, mine, :] = kv_in[core * key_heads + h]

    def bring_queries():
        bring(q_raw, write_to(q_in), True)
        swaps[key_heads].start()
        bring(g_raw, write_to(g_in), False)
        swaps[key_heads + 1].start()
        q_full[:, mine, :] = q_in[pl.ds(core * heads, heads)]
        g_full[:, mine, :] = g_in[pl.ds(core * heads, heads)]
        part[width] = jnp.zeros(part.shape[1:], part.dtype)

    def early(h):
        return inner > 1 and h in EARLY

    def lanes(h):
        return 2 if early(h) else 1

    def column(lane):
        return y if lane == 0 else inner - 1 - y

    def gather_z(s, h, lane):
        view = kv[h].at[(z - s) * inner + column(lane)]
        return remote(view, view, gz_send.at[s, h, lane], gz_recv.at[s, h, lane], up)

    def arrived_z(s, h, lane):
        view = kv[h].at[(z - s) * inner + column(lane)]
        return remote(view, view, gz_send.at[s - 1, h, lane], gz_recv.at[s - 1, h, lane], down)

    def gather_y(s, h):
        view = kv[h].at[(z - s) * inner + column(0)]
        return remote(view, view, gy_send.at[s, h], gy_recv.at[s, h], side)

    def arrived_y(s, h):
        view = kv[h].at[(z - s) * inner + column(1)]
        return remote(view, view, gy_send.at[s, h], gy_recv.at[s, h], side)

    def crosses(s, h):
        return inner > 1 and (s == 0 or not early(h))

    def sends_y(s, h):
        return (z >= s) & (y == 0) if s == 0 and not early(h) else z >= s

    def takes_y(s, h):
        return (z >= s) & (y == 1) if s == 0 and not early(h) else z >= s

    def forward(s, h):
        if s == 0:
            swaps[h].wait_recv()
            if early(h):
                gather_y(0, h).start()
        for lane in range(lanes(h)):
            if s > 0:

                @pl.when(z >= s)
                def _():
                    arrived_z(s, h, lane).wait_recv()

            elif lane == 1:
                arrived_y(0, h).wait_recv()

            @pl.when((z >= s) & (z < outer - 1))
            def _():
                gather_z(s, h, lane).start()

        if crosses(s, h) and not early(h):

            @pl.when(sends_y(s, h))
            def _():
                gather_y(s, h).start()

    def attend(h):
        if inner > 1 and not early(h):
            for s in range(outer):

                @pl.when(takes_y(s, h))
                def _():
                    arrived_y(s, h).wait_recv()

        if h == 0:
            swaps[key_heads].wait_recv()
            swaps[key_heads + 1].wait_recv()
        first = h * group
        for entry in range(width):
            block = jnp.maximum(list_ref[entry], 0)
            k_all[pl.ds(entry * BLOCK, BLOCK), :] = kv[h][block, 0]
            v_all[pl.ds(entry * BLOCK, BLOCK), :] = kv[h][block, 1]
        q = q_full[pl.ds(first, group)].reshape(rows, depth)
        g = g_full[pl.ds(first, group)].reshape(rows, depth)
        kk, vv = k_all[...], v_all[...]
        score = lax.dot_general(kk, q, nt, preferred_element_type=f32) * scale
        prob_grad = lax.dot_general(vv, g, nt, preferred_element_type=f32)
        key_row = lax.broadcasted_iota(jnp.int32, (BLOCK, rows), 0)
        query_row = lax.broadcasted_iota(jnp.int32, (BLOCK, rows), 1) % BLOCK
        causal = key_row <= query_row
        pieces = []
        for entry in range(width):
            block = list_ref[entry]
            allowed = jnp.logical_and(block >= 0, jnp.logical_or(block != me, causal))
            pieces.append(jnp.where(allowed, score[entry * BLOCK : (entry + 1) * BLOCK], NEG_FILL))
        score = jnp.concatenate(pieces, axis=0)
        best = jnp.max(score, axis=0, keepdims=True)
        weights = jnp.exp(score - best)
        inverse = 1.0 / jnp.sum(weights, axis=0, keepdims=True)
        out_t = jnp.dot(vv.T, weights.astype(low), preferred_element_type=f32) * inverse
        out_low = out_t.astype(low)
        out_full[pl.ds(first, group)] = out_t.T.astype(low).reshape(group, BLOCK, depth)
        delta = jnp.sum(g.astype(f32).T * out_low.astype(f32), axis=0, keepdims=True)
        prob = weights * inverse
        score_grad = (prob * (prob_grad - delta)).astype(low)
        value_part = jnp.dot(prob.astype(low), g, preferred_element_type=f32).astype(low)
        key_part = (jnp.dot(score_grad, q, preferred_element_type=f32) * scale).astype(low)
        for entry in range(width):
            part[entry, 0] = key_part[entry * BLOCK : (entry + 1) * BLOCK]
            part[entry, 1] = value_part[entry * BLOCK : (entry + 1) * BLOCK]

        def place(block):
            slot = jnp.int32(width)
            for entry in range(width):
                slot = jnp.where(list_ref[entry] == block, entry, slot)
            return slot

        def spread(zd):
            if inner > 1 and not early(h):

                @pl.when((zd < z) | ((zd == z) & (y == 1)))
                def _():
                    y_send[h, zd] = part[place(zd * inner + column(1))]
                    reduce_y(zd, h).start()

            for lane in range(lanes(h)):
                own[h, zd, lane] = part[place(zd * inner + column(lane))]

        repeat(outer, spread)
        qg = (jnp.dot(kk.T, score_grad, preferred_element_type=f32) * scale).T
        qg = qg.reshape(group, BLOCK, depth)
        half = depth // 2
        swapped = jnp.concatenate([qg[..., half:], qg[..., :half]], axis=-1)
        qg_full[pl.ds(first, group)] = (qg * cos_ref[...][None] - swapped * sin_ref[...][None]).astype(low)
        for copy in homeward(h):
            copy.start()
        out_home[pl.ds(core * heads + first, group)] = out_full[pl.ds(first, group), mine, :]
        qg_home[pl.ds(core * heads + first, group)] = qg_full[pl.ds(first, group), mine, :]

    def homeward(h):
        source, target = pl.ds(h * group, group), pl.ds(core * heads + h * group, group)
        a, b = key_heads + 2 + h, 2 * key_heads + 2 + h
        return (
            remote(out_full.at[source, theirs, :], out_home.at[target], core_send.at[a], core_recv.at[a], twin),
            remote(qg_full.at[source, theirs, :], qg_home.at[target], core_send.at[b], core_recv.at[b], twin),
        )

    def reduce_y(zd, h):
        return remote(y_send.at[h, zd], y_part.at[h, zd], ry_send.at[zd, h], ry_recv.at[zd, h], side)

    def reduce_z(zd, h, lane):
        return remote(
            z_send.at[h, zd, lane], z_part.at[h, zd, lane], rz_send.at[zd, h, lane], rz_recv.at[zd, h, lane], down
        )

    def reduce(h):
        def one(zd):
            for lane in reversed(range(lanes(h))):

                @pl.when(zd <= z)
                def _():
                    acc[...] = own[h, zd, lane].astype(f32)

                    if inner > 1 and not early(h):

                        @pl.when((zd < z) | (y == 0))
                        def _():
                            reduce_y(zd, h).wait_recv()
                            acc[...] += y_part[h, zd].astype(f32)

                    @pl.when(z < outer - 1)
                    def _():
                        reduce_z(zd, h, lane).wait_recv()
                        acc[...] += z_part[h, zd, lane].astype(f32)

                    @pl.when(zd < z)
                    def _():
                        z_send[h, zd, lane] = acc[...].astype(low)
                        reduce_z(zd, h, lane).start()

                    @pl.when(zd == z)
                    def _():
                        if lane == 1:
                            y_send[h, zd] = acc[...].astype(low)
                            reduce_y(zd, h).start()
                        else:
                            total_kv[h] = acc[...]

        repeat(outer, one)

    def settle(h):
        if early(h):
            reduce_y(z, h).wait_recv()
            total_kv[h] += y_part[h, z].astype(f32)

    moves = sorted((h + SKEW * s, s, h) for h in range(key_heads) for s in range(outer))
    ends = [moves.index((h + SKEW * (outer - 1), outer - 1, h)) for h in range(key_heads)]
    ready = [min(end + LAG, len(moves) - 1) for end in ends]
    for step, (_, s, h) in enumerate(moves):
        forward(s, h)
        if step == key_heads - 1:
            bring_queries()
        for done in range(key_heads):
            if ready[done] == step:
                attend(done)
                if done >= 1:
                    reduce(done - 1)
    for h in range(key_heads):
        for copy in homeward(h):
            copy.wait()
    take(lambda place: out_home[:, place, :], out_raw)
    take(lambda place: qg_home[:, place, :], qg_raw)
    reduce(key_heads - 1)
    for h in range(key_heads):
        settle(h)

    key_total = total_kv[:, 0]
    half = depth // 2
    swapped = jnp.concatenate([key_total[..., half:], key_total[..., :half]], axis=-1)
    kvg[:, 0] = (key_total * cos_ref[...][None] - swapped * sin_ref[...][None]).astype(low)
    kvg[:, 1] = total_kv[:, 1].astype(low)
    final = 3 * key_heads + 2
    target = pl.ds(core * key_heads, key_heads)
    closing = remote(kvg.at[:, :, theirs, :], kvg_home.at[target], core_send.at[final], core_recv.at[final], twin)
    closing.start()
    kvg_home[target] = kvg[:, :, mine, :]

    for copy in swaps:
        copy.wait_send()
    for h in range(key_heads):
        for s in range(outer):

            for lane in range(lanes(h)):

                @pl.when((z >= s) & (z < outer - 1))
                def _():
                    gather_z(s, h, lane).wait_send()

                @pl.when(s < z)
                def _():
                    reduce_z(s, h, lane).wait_send()

            if crosses(s, h):

                @pl.when(sends_y(s, h))
                def _():
                    gather_y(s, h).wait_send()

            if inner > 1 and not early(h):

                @pl.when((s < z) | ((s == z) & (y == 1)))
                def _():
                    reduce_y(s, h).wait_send()

        if early(h):
            reduce_y(z, h).wait_send()
    closing.wait()
    take(lambda place: kvg_home[:, 0, place, :], kg_raw)
    take(lambda place: kvg_home[:, 1, place, :], vg_raw)


def flow(blocks, list_row, q, k, v, g, cosine, sine):
    tokens, heads, depth = q.shape
    key_heads = k.shape[1] // 2
    group = heads // k.shape[1]
    width = list_row.shape[0]
    inner = 2 if blocks == 8 else 1
    outer = blocks // inner
    low, f32 = jnp.bfloat16, jnp.float32
    vmem, dma = pltpu.VMEM, pltpu.SemaphoreType.DMA
    whole = pl.BlockSpec(memory_space=pltpu.VMEM)
    half_heads = (heads // 2, BLOCK, depth)
    tile = (2, BLOCK, depth)
    sided = (key_heads, outer if inner > 1 else 1) + tile
    flags = (outer, key_heads)
    scratch = [vmem((blocks,) + tile, low)] * key_heads
    home = [vmem((heads, tokens, depth), low)] * 2 + [vmem((2 * key_heads, 2, tokens, depth), low)]
    scratch += home + home + [vmem(half_heads, low)] * 4
    scratch += [vmem((key_heads,) + tile, low)]
    scratch += [vmem((width * BLOCK, depth), low)] * 2
    scratch += [vmem((width + 1,) + tile, low)]
    scratch += [vmem((key_heads, outer, inner) + tile, low)]
    scratch += [vmem(sided, low)] * 2
    scratch += [vmem((key_heads, outer, inner) + tile, low)] * 2
    scratch += [vmem(tile, f32), vmem((key_heads,) + tile, f32)]
    scratch += [dma((3 * key_heads + 3,))] * 2
    scratch += [dma(flags + (inner,))] * 2 + [dma(flags)] * 4 + [dma(flags + (inner,))] * 2
    return pl.pallas_call(
        functools.partial(flow_kernel, blocks, inner, width, group, 1.0 / math.sqrt(depth)),
        in_specs=[pl.BlockSpec(memory_space=pltpu.SMEM)] + [whole] * 6,
        out_specs=[whole] * 4,
        out_shape=[jax.ShapeDtypeStruct(x.shape, low) for x in (q, q, k, k)],
        scratch_shapes=scratch,
        compiler_params=pltpu.CompilerParams(
            collective_id=0, has_side_effects=True, vmem_limit_bytes=60 << 20
        ),
        name="flow",
    )(list_row, q, k, v, g, cosine, sine)


def quad_kernel(
    outer, width, group, scale,
    list_ref, place_ref, k_far, v_far, token_far, base_far, q_far, g_far, out_raw, qg_raw, kg_raw, vg_raw, *scratch,
):
    tokens, key_heads, depth = k_far.shape
    local = key_heads // 4
    heads = local * group
    rows = group * BLOCK
    f32, low = jnp.float32, jnp.bfloat16
    nt = (((1,), (1,)), ((), ()))
    kv = scratch[:local]
    (q_raw, g_raw, kv_in, q_in, g_in, q_full, g_full, out_full, qg_full, out_home, qg_home, kvg, kvg_home, k_all, v_all, part,
     own, z_send, z_part, acc, cos_ref, sin_ref, note,
     far_sem, note_send, note_recv, kv_send, kv_recv, q_send, q_recv, g_send, g_recv, out_send, out_recv, qg_send, qg_recv,
     home_send, home_recv, gz_send, gz_recv, rz_send, rz_recv, relay_recv, relay, pending, k_raw, v_raw, token_ref, base_ref, out_turned, slopes) = scratch[local:]

    me = lax.axis_index("blk")
    core = lax.axis_index("head")
    z, y = me // 2, me % 2
    quarter = 2 * y + core
    mesh_id = pl.DeviceIdType.MESH
    mine = pl.ds(pl.multiple_of(core * tokens, tokens), tokens)
    theirs = pl.ds(pl.multiple_of((1 - core) * tokens, tokens), tokens)
    half = depth // 2
    step_tokens = 16

    def row_of(side):
        return y if side == 0 else 1 - y

    def core_of(cross):
        return core if cross == 0 else 1 - core

    def peer(side, cross):
        return {"blk": 2 * z + row_of(side), "head": core_of(cross)}

    def quarter_of(side, cross):
        return 2 * row_of(side) + core_of(cross)

    def level(other):
        return {"blk": 2 * other + y}

    def remote(source, target, send, recv, device):
        return pltpu.make_async_remote_copy(
            src_ref=source, dst_ref=target, send_sem=send, recv_sem=recv, device_id=device, device_id_type=mesh_id
        )

    peers = ((0, 1), (1, 0), (1, 1))
    barrier = pltpu.get_barrier_semaphore()
    for side, cross in peers:
        pl.semaphore_signal(barrier, inc=1, device_id=peer(side, cross), device_id_type=mesh_id)
    for other in range(outer):

        @pl.when(z != other)
        def _():
            pl.semaphore_signal(barrier, inc=1, device_id=level(other), device_id_type=mesh_id)

    def bring_in(index, far, near):
        copy = pltpu.make_async_copy(far, near, far_sem.at[index])
        copy.start()
        return copy

    far_token, far_base = bring_in(0, token_far, token_ref), bring_in(1, base_far, base_ref)
    far_k, far_v = bring_in(2, k_far, k_raw), bring_in(3, v_far, v_raw)
    far_q, far_g = bring_in(4, q_far, q_raw), bring_in(5, g_far, g_raw)

    def angles(side, depth_of):
        first = base_ref[depth_of]
        cosine, sine = first[0:1], first[1:2]
        cos_ref[side] = token_ref[0] * cosine - token_ref[1] * sine
        sin_ref[side] = token_ref[1] * cosine + token_ref[0] * sine

    depth_here = place_ref[0] // BLOCK
    far_token.wait()
    far_base.wait()
    angles(0, depth_here)
    for entry in range(width):
        note[0, entry] = list_ref[0, entry]
    note[0, width] = depth_here

    def turn(x, place, sign):
        cosine, sine = cos_ref[0, place, :], sin_ref[0, place, :]
        swapped = pltpu.roll(x, half, x.ndim - 1)
        return x * cosine[None] + swapped * (sign * sine)[None]

    def bring(raw, write, rotate):
        for start in range(0, tokens, step_tokens):
            x = jnp.transpose(raw[start : start + step_tokens].astype(f32), (1, 0, 2))
            if rotate:
                place = pl.ds(pl.multiple_of(core * tokens + start, step_tokens), step_tokens)
                x = turn(x, place, 1.0)
            write(slice(start, start + step_tokens), x.astype(low))

    def take(read, raw):
        for start in range(0, tokens, step_tokens):
            x = read(slice(start, start + step_tokens)).astype(f32)
            raw[start : start + step_tokens] = jnp.transpose(x, (1, 0, 2)).astype(low)

    def write_to(ref, lane=None):
        def write(place, x):
            if lane is None:
                ref[:, place, :] = x
            else:
                ref[:, lane, place, :] = x

        return write

    def send_note():
        return remote(note.at[0], note.at[1], note_send, note_recv, peer(1, 0))

    def swap_kv(h, r):
        return remote(
            kv_in.at[quarter_of(*peers[r]) * local + h], kv[h].at[me, :, mine, :], kv_send.at[h, r], kv_recv.at[h, r], peer(*peers[r])
        )

    def swap_q(h, r):
        source = pl.ds(quarter_of(*peers[r]) * heads + h * group, group)
        target = q_full.at[peers[r][0], pl.ds(h * group, group), mine, :]
        return remote(q_in.at[source], target, q_send.at[h, r], q_recv.at[h, r], peer(*peers[r]))

    def swap_g(h, r):
        source = pl.ds(quarter_of(*peers[r]) * heads + h * group, group)
        target = g_full.at[peers[r][0], pl.ds(h * group, group), mine, :]
        return remote(g_in.at[source], target, g_send.at[h, r], g_recv.at[h, r], peer(*peers[r]))

    def gather_z(h, side, far):
        view = kv[h].at[2 * z + row_of(side)]
        return remote(view, view, gz_send.at[h, side, far], gz_recv.at[h, side, z], level(far))

    def arrived_z(h, side, near):
        view = kv[h].at[2 * near + row_of(side)]
        return remote(view, view, gz_send.at[h, side, near], gz_recv.at[h, side, near], level(near))

    def reduce_z(h, side, near):
        return remote(
            z_send.at[h, near, side], z_part.at[h, z, side], rz_send.at[h, side, near], rz_recv.at[h, side, z], level(near)
        )

    def returned_z(h, side, far):
        return remote(
            z_send.at[h, far, side], z_part.at[h, far, side], rz_send.at[h, side, far], rz_recv.at[h, side, far], level(far)
        )

    last, relay_level = outer - 1, outer - 2

    def upward(h, side):
        for far in reversed(range(1, outer)):

            @pl.when((z < far) & (far - z < last))
            def _():
                gather_z(h, side, far).start()

    def relayed_up(h, side):
        view = kv[h].at[row_of(side)]
        return remote(view, view, gz_send.at[h, side, 0], gz_recv.at[h, side, 0], level(last))

    def pass_up(h, side):
        @pl.when(z == relay_level)
        def _():
            arrived_z(h, side, 0).wait_recv()
            relayed_up(h, side).start()

    def relayed_down(h, side):
        return remote(
            z_send.at[h, 0, side], relay.at[h, side], rz_send.at[h, side, 0], relay_recv.at[h, side], level(relay_level)
        )

    def pass_down(h):
        for lane in (1, 0):

            @pl.when(z == relay_level)
            def _():
                relayed_down(h, lane).wait_recv()
                z_send[h, 0, lane] = (pending[h, lane] + relay[h, lane].astype(f32)).astype(low)
                reduce_z(h, lane, 0).start()

    far_k.wait()
    bring(k_raw, write_to(kv_in, 0), True)
    far_v.wait()
    bring(v_raw, write_to(kv_in, 1), False)
    pl.semaphore_wait(barrier, outer + 2)
    for h in range(local):
        for r in range(3):
            swap_kv(h, r).start()
    send_note().start()
    for h in range(local):
        kv[h][me, :, mine, :] = kv_in[quarter * local + h]
    swap_kv(0, 0).wait_recv()
    upward(0, 0)
    far_q.wait()
    bring(q_raw, write_to(q_in), True)
    for r in range(3):
        swap_q(0, r).start()
    for r in (1, 2):
        swap_kv(0, r).wait_recv()
    upward(0, 1)
    swap_kv(1, 0).wait_recv()
    upward(1, 0)
    for r in (1, 2):
        swap_kv(1, r).wait_recv()
    upward(1, 1)
    far_g.wait()
    bring(g_raw, write_to(g_in), False)
    for r in range(3):
        swap_g(0, r).start()
    for h in range(1, local):
        for r in range(3):
            swap_q(h, r).start()
            swap_g(h, r).start()
    q_full[0, :, mine, :] = q_in[pl.ds(quarter * heads, heads)]
    g_full[0, :, mine, :] = g_in[pl.ds(quarter * heads, heads)]
    for side in range(2):
        part[side, width] = jnp.zeros(part.shape[2:], part.dtype)
    send_note().wait_recv()
    angles(1, note[1, width])

    def homeward(h, side):
        copies = []
        for r in range(3):
            if peers[r][0] != side:
                continue
            place = mine if peers[r][1] == 0 else theirs
            source = pl.ds(h * group, group)
            target = pl.ds(quarter * heads + h * group, group)
            copies.append(
                remote(out_full.at[side, source, place, :], out_home.at[target], out_send.at[h, r], out_recv.at[h, r], peer(*peers[r]))
            )
            copies.append(
                remote(qg_full.at[side, source, place, :], qg_home.at[target], qg_send.at[h, r], qg_recv.at[h, r], peer(*peers[r]))
            )
        return copies

    def attend(h, side):
        if side == 1:
            for near in range(outer - 1):
                for lane in range(2):

                    @pl.when((near < z) & ((near > 0) | (z != relay_level)))
                    def _():
                        arrived_z(h, lane, near).wait_recv()

            for r in range(3):
                swap_q(h, r).wait_recv()
                swap_g(h, r).wait_recv()
        block_here = 2 * z + row_of(side)
        first = h * group
        for entry in range(width):
            block = jnp.maximum(note[side, entry], 0)
            k_all[side, pl.ds(entry * BLOCK, BLOCK), :] = kv[h][block, 0]
            v_all[pl.ds(entry * BLOCK, BLOCK), :] = kv[h][block, 1]
        q = q_full[side, pl.ds(first, group)].reshape(rows, depth)
        g = g_full[side, pl.ds(first, group)].reshape(rows, depth)
        kk, vv = k_all[side], v_all[...]
        score = lax.dot_general(kk, q, nt, preferred_element_type=f32)
        prob_grad = lax.dot_general(vv, g, nt, preferred_element_type=f32)
        key_row = lax.broadcasted_iota(jnp.int32, (BLOCK, rows), 0)
        query_row = lax.broadcasted_iota(jnp.int32, (BLOCK, rows), 1) % BLOCK
        causal = key_row <= query_row
        pieces = []
        for entry in range(width):
            block = note[side, entry]
            allowed = jnp.logical_and(block >= 0, jnp.logical_or(block != block_here, causal))
            pieces.append(jnp.where(allowed, score[entry * BLOCK : (entry + 1) * BLOCK], NEG_FILL))
        score = jnp.concatenate(pieces, axis=0)
        best = jnp.max(score, axis=0, keepdims=True)
        weights = jnp.exp2((score - best) * (scale * math.log2(math.e)))
        inverse = 1.0 / jnp.sum(weights, axis=0, keepdims=True)
        out_t = jnp.dot(vv.T, weights.astype(low), preferred_element_type=f32) * inverse
        out_low = out_t.astype(low)
        out_turned[side] = out_low
        delta = jnp.sum(g.astype(f32).T * out_low.astype(f32), axis=0, keepdims=True)
        prob = weights * inverse
        score_grad = (prob * (prob_grad - delta)).astype(low)
        slopes[side] = score_grad
        value_part = jnp.dot(prob.astype(low), g, preferred_element_type=f32).astype(low)
        key_part = (jnp.dot(score_grad, q, preferred_element_type=f32) * scale).astype(low)
        for entry in range(width):
            part[side, entry, 0] = key_part[entry * BLOCK : (entry + 1) * BLOCK]
            part[side, entry, 1] = value_part[entry * BLOCK : (entry + 1) * BLOCK]

    def finish(h, side):
        first = h * group
        out_full[side, pl.ds(first, group)] = out_turned[side].astype(f32).T.astype(low).reshape(group, BLOCK, depth)
        qg = (jnp.dot(k_all[side].T, slopes[side], preferred_element_type=f32) * scale).T
        qg = qg.reshape(group, BLOCK, depth)
        swapped = jnp.concatenate([qg[..., half:], qg[..., :half]], axis=-1)
        qg_full[side, pl.ds(first, group)] = (qg * cos_ref[side][None] - swapped * sin_ref[side][None]).astype(low)
        for copy in homeward(h, side):
            copy.start()
        if side == 0:
            target = pl.ds(quarter * heads + first, group)
            out_home[target] = out_full[0, pl.ds(first, group), mine, :]
            qg_home[target] = qg_full[0, pl.ds(first, group), mine, :]

    def slot_of(side, block):
        slot = jnp.int32(width)
        for entry in range(width):
            slot = jnp.where(note[side, entry] == block, entry, slot)
        return slot

    def spread(h):
        for near in range(outer):
            for lane in (1, 0):

                @pl.when(near <= z)
                def _():
                    block = 2 * near + row_of(lane)
                    total = part[0, slot_of(0, block)].astype(f32) + part[1, slot_of(1, block)].astype(f32)

                    @pl.when((near < z) & ((near > 0) | (z < relay_level)))
                    def _():
                        z_send[h, near, lane] = total.astype(low)
                        reduce_z(h, lane, near).start()

                    if near == 0:

                        @pl.when(z == relay_level)
                        def _():
                            pending[h, lane] = total

                        @pl.when(z == last)
                        def _():
                            z_send[h, near, lane] = total.astype(low)
                            relayed_down(h, lane).start()

                    @pl.when(near == z)
                    def _():
                        own[h, lane] = total

    def kv_home(h, r):
        side, cross = peers[r]
        place = mine if cross == 0 else theirs
        return remote(
            kvg.at[h, side, :, place, :], kvg_home.at[quarter * local + h], home_send.at[h, r], home_recv.at[h, r], peer(side, cross)
        )

    def settle(h):
        for lane in (1, 0):
            acc[...] = own[h, lane]
            for far in range(1, outer):

                @pl.when((z < far) & (far - z < last))
                def _():
                    returned_z(h, lane, far).wait_recv()
                    acc[...] += z_part[h, far, lane].astype(f32)

            key_total = acc[0]
            swapped = jnp.concatenate([key_total[..., half:], key_total[..., :half]], axis=-1)
            kvg[h, lane, 0] = (key_total * cos_ref[lane] - swapped * sin_ref[lane]).astype(low)
            kvg[h, lane, 1] = acc[1].astype(low)
            for r in range(3):
                if peers[r][0] == lane:
                    kv_home(h, r).start()
        kvg_home[quarter * local + h] = kvg[h, 0, :, mine, :]

    pass_up(0, 0)
    pass_up(0, 1)
    for h in range(local):
        attend(h, 1)
        if h + 1 < local:
            pass_up(h + 1, 0)
        if h > 0:
            pass_down(h - 1)
        attend(h, 0)
        if h + 1 < local:
            pass_up(h + 1, 1)
        spread(h)
        finish(h, 1)
        finish(h, 0)
    pass_down(local - 1)
    for h in range(local - 1):
        settle(h)
    for h in range(local):
        for side in range(2):
            for copy in homeward(h, side):
                copy.wait()
    take(lambda place: out_home[:, place, :], out_raw)
    take(lambda place: qg_home[:, place, :], qg_raw)
    settle(local - 1)

    send_note().wait_send()
    for h in range(local):
        for r in range(3):
            swap_kv(h, r).wait_send()
            swap_q(h, r).wait_send()
            swap_g(h, r).wait_send()
        for side in range(2):
            for far in range(1, outer):

                @pl.when((z < far) & (far - z < last))
                def _():
                    gather_z(h, side, far).wait_send()

            @pl.when(z == relay_level)
            def _():
                relayed_up(h, side).wait_send()

            for near in range(outer - 1):

                @pl.when((near < z) & (z - near < last))
                def _():
                    reduce_z(h, side, near).wait_send()

            @pl.when(z == last)
            def _():
                relayed_down(h, side).wait_send()

    for h in range(local):
        for r in range(3):
            kv_home(h, r).wait()
    take(lambda place: kvg_home[:, 0, place, :], kg_raw)
    take(lambda place: kvg_home[:, 1, place, :], vg_raw)


def store_kernel(*refs):
    done = refs[8]
    copies = [pltpu.make_async_copy(refs[index], refs[4 + index], done.at[index]) for index in range(4)]
    for copy in copies:
        copy.start()
    for copy in copies:
        copy.wait()


def angle_tables(width, depth):
    half = depth // 2
    frequency = ROPE_BASE ** (-2.0 * np.arange(half) / depth)

    def pair(place):
        angle = place[:, None] * frequency[None, :]
        cosine, sine = np.cos(angle), np.sin(angle)
        return np.stack([np.concatenate([cosine, cosine], -1), np.concatenate([-sine, sine], -1)]).astype(np.float32)

    token = pair(np.arange(BLOCK, dtype=np.float64))
    base = pair(np.arange(width, dtype=np.float64) * BLOCK)
    return token, np.moveaxis(base, 0, 1)


def quad(blocks, list_rows, places, q, k, v, g):
    tokens, heads, depth = q.shape
    key_heads = k.shape[1]
    group = heads // key_heads
    local = key_heads // 4
    width = list_rows.shape[1]
    outer = blocks // 2
    low, f32 = jnp.bfloat16, jnp.float32
    vmem, dma = pltpu.VMEM, pltpu.SemaphoreType.DMA
    whole = pl.BlockSpec(memory_space=pltpu.VMEM)
    scalar = pl.BlockSpec(memory_space=pltpu.SMEM)
    distant = pl.BlockSpec(memory_space=pl.ANY)
    token, base = angle_tables(width, depth)
    tile = (2, BLOCK, depth)
    full = (2, local * group, BLOCK, depth)
    scratch = [vmem((blocks,) + tile, low)] * local
    scratch += [vmem(q.shape, low)] * 2
    scratch += [vmem((key_heads, 2, tokens, depth), low)] + [vmem((heads, tokens, depth), low)] * 2
    scratch += [vmem(full, low)] * 4 + [vmem((heads, tokens, depth), low)] * 2
    scratch += [vmem((local, 2) + tile, low), vmem((key_heads, 2, tokens, depth), low)]
    scratch += [vmem((2, width * BLOCK, depth), low), vmem((width * BLOCK, depth), low)]
    scratch += [vmem((2, width + 1) + tile, low), vmem((local, 2) + tile, f32)]
    scratch += [vmem((local, outer, 2) + tile, low)] * 2
    scratch += [vmem(tile, f32)] + [vmem((2, BLOCK, depth), f32)] * 2
    scratch += [pltpu.SMEM((2, 2 * width), jnp.int32)]
    scratch += [dma((6,)), dma, dma] + [dma((local, 3))] * 12 + [dma((local, 2, outer))] * 4
    scratch += [dma((local, 2)), vmem((local, 2) + tile, low), vmem((local, 2) + tile, f32)]
    scratch += [vmem(k.shape, low)] * 2 + [vmem(token.shape, f32), vmem(base.shape, f32)]
    scratch += [vmem((2, depth, group * BLOCK), low), vmem((2, width * BLOCK, group * BLOCK), low)]
    results = pl.pallas_call(
        functools.partial(quad_kernel, outer, width, group, 1.0 / math.sqrt(depth)),
        in_specs=[scalar] * 2 + [distant] * 6,
        out_specs=[whole] * 4,
        out_shape=[vmem(x.shape, low) for x in (q, q, k, k)],
        scratch_shapes=scratch,
        compiler_params=pltpu.CompilerParams(
            collective_id=1, has_side_effects=True, vmem_limit_bytes=60 << 20
        ),
        name="quad_flow",
    )(list_rows, places, k, v, jnp.asarray(token), jnp.asarray(base), q, g)
    return pl.pallas_call(
        store_kernel,
        in_specs=[distant] * 4,
        out_specs=[distant] * 4,
        out_shape=[jax.ShapeDtypeStruct(x.shape, low) for x in (q, q, k, k)],
        scratch_shapes=[dma((4,))],
        compiler_params=pltpu.CompilerParams(has_side_effects=True, vmem_limit_bytes=4 << 20),
        name="store",
    )(*results)


def body(blocks, queries, keys, values, out_grad, block_list, positions):
    tokens, _, depth = queries.shape
    if blocks == 8:
        return tuple(quad(blocks, block_list, positions, queries, keys, values, out_grad))
    base = positions[0] - lax.axis_index("head") * tokens
    cosine, sine = tables(base + jnp.arange(BLOCK, dtype=jnp.int32), depth)
    return tuple(flow(blocks, block_list[0], queries, keys, values, out_grad, cosine, sine))


def solution(mesh):
    spec = P(("groups", "blk", "head"), None, None)
    in_specs = (spec, spec, spec, spec, P(("groups", "blk"), None), P(("groups", "blk", "head")))
    run = functools.partial(body, mesh.shape["blk"])
    return jax.shard_map(run, mesh=mesh, in_specs=in_specs, out_specs=(spec,) * 4, check_vma=False)
```
